512 devices in a mesh: wide: 64 (over z, y_hi, core), narrow: 8 (over x, y_lo).
Axes of the slice: x: 4, y: 4 (y_hi: 2, y_lo: 2; y = y_hi * 2 + y_lo), z: 16, core: 2. Of those that a mesh axis runs over, the one named last changes fastest.
Arguments:
- tokens: bfloat16 [512, 8192], P('wide', 'narrow'), may hold values from -6 to 6
- cotangent: bfloat16 [512, 8192], P('wide', 'narrow'), may hold values from -2.390625 to 2.390625
- gate_vals: bfloat16 [8, 64, 12, 128, 128], P('narrow', 'wide'), may hold values from -0.125 to 0.125
- up_vals: bfloat16 [8, 64, 12, 128, 128], P('narrow', 'wide'), may hold values from -0.125 to 0.125
- gu_index: int32 [8, 64, 12], P('narrow', 'wide'), may hold values from 0 to 15, as said below
- gu_count: int32 [8, 64], P('narrow', 'wide'), may hold values from 1 to 12, as said below
- down_vals: bfloat16 [64, 8, 12, 128, 128], P('wide', 'narrow'), may hold values from -0.09375 to 0.09375
- down_index: int32 [64, 8, 12], P('wide', 'narrow'), may hold values from 0 to 15, as said below
- down_count: int32 [64, 8], P('wide', 'narrow'), may hold values from 1 to 12, as said below
Outputs:
- d_tokens: bfloat16 [512, 8192], P('wide', 'narrow')
- gate_grad: bfloat16 [8, 64, 12, 128, 128], P('narrow', 'wide')
- up_grad: bfloat16 [8, 64, 12, 128, 128], P('narrow', 'wide')
- down_grad: bfloat16 [64, 8, 12, 128, 128], P('wide', 'narrow')
The draws below stay inside these ranges and needn't reach their ends.
Inputs may be any that keep to these rules, and one draw needn't show every extreme that they name: `gu_index`: within each tile all 12 entries are different. `gu_count`: some tile has exactly 12 live slots. `down_index`: within each tile all 12 entries are different. `down_count`: some tile has exactly 12 live slots.
All inputs are finite; a program needn't handle non-finite values.
Results may differ from the reference program's by a relative error of at most 0.005.
Values may be sent and summed in bfloat16 or wider, within the bound.
A program may use at most 64 MiB of HBM per device.

```python
import jax
import jax.numpy as jnp
from jax import lax

D = 8192
FF = 16384
BLOCK = 128
TOKENS = 512
D_SPLIT = 8
F_SPLIT = 64
D_BLOCKS = 8
F_BLOCKS = 2
SLOTS = 12


def tile_indices(key, tiles_a, tiles_b):
    keys = jax.random.split(key, tiles_a * tiles_b)
    perms = jax.vmap(lambda single: jax.random.permutation(single, D_BLOCKS * F_BLOCKS)[:SLOTS])(keys)
    return perms.reshape(tiles_a, tiles_b, SLOTS).astype(jnp.int32)


def tile_counts(key, tiles_a, tiles_b):
    total = tiles_a * tiles_b
    counts = jax.random.randint(key, (total,), 1, 2 * (D_BLOCKS * F_BLOCKS // 4), dtype=jnp.int32)
    fullest = jax.random.randint(jax.random.fold_in(key, 5), (), 0, total, dtype=jnp.int32)
    counts = jnp.where(jnp.arange(total, dtype=jnp.int32) == fullest, SLOTS, counts)
    return counts.reshape(tiles_a, tiles_b).astype(jnp.int32)


def draw_gu_index(key, part):
    return tile_indices(jax.random.fold_in(key, 11), D_SPLIT, F_SPLIT)


def draw_gu_count(key, part):
    return tile_counts(jax.random.fold_in(key, 23), D_SPLIT, F_SPLIT)


def draw_down_index(key, part):
    return tile_indices(jax.random.fold_in(key, 37), F_SPLIT, D_SPLIT)


def draw_down_count(key, part):
    return tile_counts(jax.random.fold_in(key, 41), F_SPLIT, D_SPLIT)


def level_of(stream_key, dims, shards, least, top_value):
    def one(axis_at, parts):
        draws = jax.random.uniform(jax.random.fold_in(jax.random.fold_in(stream_key, 6), axis_at), (parts,), jnp.float32, least / len(shards), top_value / len(shards))
        return jnp.repeat(jnp.exp(draws), dims[axis_at] // parts).reshape((-1,) + (1,) * (len(dims) - axis_at - 1))

    factor_of = one(*shards[0])
    for cut in shards[1:]:
        factor_of = factor_of * one(*cut)
    return factor_of


def centred(rng, shape, spread, reach, pieces=(), held_as=jnp.bfloat16):
    values = jax.random.normal(rng, shape, jnp.float32) * spread
    if len(pieces) > 0:
        values = level_of(rng, shape, pieces, -0.22, 0.18) * values
    return jnp.clip(values, min=-reach, max=reach).astype(held_as)


def setup_inputs(seed: int = 0) -> dict:
    arg_keys = jax.random.split(jax.random.key(seed), 10)
    return {
        "tokens": centred(arg_keys[0], (TOKENS, D), 1.0, 6.0, ((0, 64), (1, 8))),
        "cotangent": centred(arg_keys[1], (TOKENS, D), 0.4, 2.390625, ((0, 64), (1, 8))),
        "gate_vals": centred(arg_keys[2], (D_SPLIT, F_SPLIT, SLOTS, BLOCK, BLOCK), (D // 4) ** -0.5, 0.125, ((0, 8), (1, 64))),
        "up_vals": centred(arg_keys[3], (D_SPLIT, F_SPLIT, SLOTS, BLOCK, BLOCK), (D // 4) ** -0.5, 0.125, ((0, 8), (1, 64))),
        "gu_index": draw_gu_index(jax.random.fold_in(arg_keys[9], 71), 0),
        "gu_count": draw_gu_count(jax.random.fold_in(arg_keys[9], 71), 0),
        "down_vals": centred(arg_keys[6], (F_SPLIT, D_SPLIT, SLOTS, BLOCK, BLOCK), (FF // 4) ** -0.5, 0.09375, ((0, 64), (1, 8))),
        "down_index": draw_down_index(jax.random.fold_in(arg_keys[9], 71), 0),
        "down_count": draw_down_count(jax.random.fold_in(arg_keys[9], 71), 0),
    }


def place_table(slot_ids, live_count, blocks_total):
    slots_total = slot_ids.shape[2]
    alive = (jnp.arange(slots_total, dtype=jnp.int32)[None, None, :] < live_count[:, :, None]).astype(jnp.float32)
    table = (slot_ids[:, :, :, None] == jnp.arange(blocks_total, dtype=jnp.int32)[None, None, None, :]).astype(jnp.float32)
    return table * alive[:, :, :, None]


def unpack_tiles(tile_values, slot_ids, live_count, row_blocks, col_blocks):
    tiles_a = tile_values.shape[0]
    tiles_b = tile_values.shape[1]
    block_size = tile_values.shape[3]
    placer = place_table(slot_ids, live_count, row_blocks * col_blocks)
    blocks = jnp.einsum("abst,absij->abtij", placer, tile_values.astype(jnp.float32), precision=lax.Precision.HIGHEST)
    blocks = blocks.reshape(tiles_a, tiles_b, row_blocks, col_blocks, block_size, block_size)
    dense = blocks.transpose(0, 2, 4, 1, 3, 5).reshape(tiles_a * row_blocks * block_size, tiles_b * col_blocks * block_size)
    return dense.astype(jnp.bfloat16)


def pack_tiles(dense, slot_ids, live_count, row_blocks, col_blocks, block_size):
    tiles_a = slot_ids.shape[0]
    tiles_b = slot_ids.shape[1]
    blocks = dense.reshape(tiles_a, row_blocks, block_size, tiles_b, col_blocks, block_size).transpose(0, 3, 1, 4, 2, 5)
    blocks = blocks.reshape(tiles_a, tiles_b, row_blocks * col_blocks, block_size, block_size)
    placer = place_table(slot_ids, live_count, row_blocks * col_blocks)
    picked = jnp.einsum("abst,abtij->absij", placer, blocks, precision=lax.Precision.HIGHEST)
    return picked.astype(jnp.bfloat16)


def reference(tokens, cotangent, gate_vals, up_vals, gu_index, gu_count, down_vals, down_index, down_count):
    block_size = gate_vals.shape[-1]
    gate_weight = unpack_tiles(gate_vals, gu_index, gu_count, D_BLOCKS, F_BLOCKS)
    up_weight = unpack_tiles(up_vals, gu_index, gu_count, D_BLOCKS, F_BLOCKS)
    down_weight = unpack_tiles(down_vals, down_index, down_count, F_BLOCKS, D_BLOCKS)
    gate_out = jnp.dot(tokens, gate_weight, preferred_element_type=jnp.float32)
    up_out = jnp.dot(tokens, up_weight, preferred_element_type=jnp.float32)
    sigmoid_g = jax.nn.sigmoid(gate_out)
    hidden = (gate_out * sigmoid_g * up_out).astype(jnp.bfloat16)
    d_hidden = jnp.dot(cotangent, down_weight.T, preferred_element_type=jnp.float32)
    d_gate = (d_hidden * up_out * sigmoid_g * (1.0 + gate_out * (1.0 - sigmoid_g))).astype(jnp.bfloat16)
    d_up = (d_hidden * gate_out * sigmoid_g).astype(jnp.bfloat16)
    d_tokens = jnp.dot(d_gate, gate_weight.T, preferred_element_type=jnp.float32) + jnp.dot(d_up, up_weight.T, preferred_element_type=jnp.float32)
    d_tokens = d_tokens.astype(jnp.bfloat16)
    gate_dense = jnp.dot(tokens.T, d_gate, preferred_element_type=jnp.float32)
    gate_grad = pack_tiles(gate_dense, gu_index, gu_count, D_BLOCKS, F_BLOCKS, block_size)
    up_dense = jnp.dot(tokens.T, d_up, preferred_element_type=jnp.float32)
    up_grad = pack_tiles(up_dense, gu_index, gu_count, D_BLOCKS, F_BLOCKS, block_size)
    down_dense = jnp.dot(hidden.T, cotangent, preferred_element_type=jnp.float32)
    down_grad = pack_tiles(down_dense, down_index, down_count, F_BLOCKS, D_BLOCKS, block_size)
    return (d_tokens, gate_grad, up_grad, down_grad)
```

```python
import jax
import jax.numpy as jnp
from jax import lax
from jax.experimental import pallas as pl
from jax.experimental.pallas import tpu as pltpu
from jax.sharding import PartitionSpec as P

MESH = pl.DeviceIdType.MESH
VMEM = pl.BlockSpec(memory_space=pltpu.VMEM)
SMEM = pl.BlockSpec(memory_space=pltpu.SMEM)
F32 = jnp.float32
BF16 = jnp.bfloat16

Z = 16
N = 8
B = 128


def wide_place():
    w = lax.axis_index("wide")
    return w // 4, (w // 2) % 2, w % 2


def wide_at(z, y, c):
    return ((z + Z) % Z * 2 + y) * 2 + c


def greet(axis, peers):
    barrier = pltpu.get_barrier_semaphore()
    for peer in peers:
        pl.semaphore_signal(barrier, inc=1, device_id={axis: peer}, device_id_type=MESH)
    pl.semaphore_wait(barrier, len(peers))


def send(axis, peer, src, dst, send_sem, recv_sem):
    copy = pltpu.make_async_remote_copy(
        src_ref=src,
        dst_ref=dst,
        send_sem=send_sem,
        recv_sem=recv_sem,
        device_id={axis: peer},
        device_id_type=MESH,
    )
    copy.start()
    return copy


def gather_kernel(mine, out, own_sem, y_sem, z_send, z_recv, c_send, c_recv):
    z, y, c = wide_place()
    right, left = wide_at(z + 1, y, c), wide_at(z - 1, y, c)
    across, partner = wide_at(z, 1 - y, c), wide_at(z, y, 1 - c)
    greet("wide", (right, left, across, partner))
    me = wide_at(z, y, c)
    rows = (y, 1 - y)
    ycopy = send("wide", across, mine, out.at[me], y_sem.at[0], y_sem.at[1])
    own = pltpu.make_async_copy(mine, out.at[me], own_sem)
    own.start()
    sent = [ycopy]
    cores = []

    def pass_on(src, slot):
        k = len(cores)
        cores.append(send("wide", partner, src, out.at[slot], c_send.at[k], c_recv.at[k]))

    last = {}
    for s in range(1, 10):
        for q in (0, 1):
            for d in (0, 1):
                steps = 8 - d
                if s > steps + 1:
                    continue
                origin = z - (s - 1) if d == 0 else z + (s - 1)
                slot = wide_at(origin, rows[q], c)
                src = out.at[slot]
                if s == 1:
                    if q == 0:
                        src = mine
                    elif d == 0:
                        ycopy.wait_recv()
                else:
                    last[d, q].wait_recv()
                if s <= steps:
                    k = (d * 2 + q) * 8 + s - 1
                    last[d, q] = send(
                        "wide",
                        right if d == 0 else left,
                        src,
                        out.at[slot],
                        z_send.at[k],
                        z_recv.at[k],
                    )
                    sent.append(last[d, q])
                if s > 1 or d == 0:
                    pass_on(src, slot)
    own.wait()
    for copy in cores:
        copy.wait_recv()
    for copy in sent + cores:
        copy.wait_send()


def gather_wide(mine):
    return pl.pallas_call(
        gather_kernel,
        out_shape=jax.ShapeDtypeStruct((4 * Z,) + mine.shape, mine.dtype),
        in_specs=[VMEM],
        out_specs=VMEM,
        scratch_shapes=[
            pltpu.SemaphoreType.DMA,
            pltpu.SemaphoreType.DMA((2,)),
            pltpu.SemaphoreType.DMA((32,)),
            pltpu.SemaphoreType.DMA((32,)),
            pltpu.SemaphoreType.DMA((32,)),
            pltpu.SemaphoreType.DMA((32,)),
        ],
        compiler_params=pltpu.CompilerParams(collective_id=0, has_side_effects=True),
        name="gather_wide",
    )(mine)


def forward_kernel(
    gu_index, gu_count, down_index, down_count, got, gate, up, down, part, wgu, wd, xs, dys
):
    wgu[...] = jnp.zeros_like(wgu)
    wd[...] = jnp.zeros_like(wd)
    for s in range(gate.shape[0]):

        @pl.when(s < gu_count[0])
        def _():
            at = gu_index[s]
            row = pl.multiple_of((at // 2) * B, B)
            col = pl.multiple_of((at % 2) * B, B)
            wgu[pl.ds(row, B), pl.ds(col, B)] = gate[s]
            wgu[pl.ds(row, B), pl.ds(2 * B + col, B)] = up[s]

        @pl.when(s < down_count[0])
        def _():
            at = down_index[s]
            row = pl.multiple_of((at // 8) * B, B)
            col = pl.multiple_of((at % 8) * B, B)
            wd[pl.ds(row, B), pl.ds(col, B)] = down[s]

    @pl.loop(0, 4)
    def _(i):
        rows = pl.ds(pl.multiple_of(i * B, B), B)
        some = pl.ds(i * (B // 8), B // 8)
        x = got[some, 0].astype(F32).reshape(B, -1).astype(BF16)
        dy = got[some, 1].astype(F32).reshape(B, -1).astype(BF16)
        xs[rows, :] = x
        dys[rows, :] = dy
        part[rows, : 4 * B] = jnp.dot(x, wgu[...], preferred_element_type=F32)
        part[rows, 4 * B :] = lax.dot_general(
            dy, wd[...], (((1,), (1,)), ((), ())), preferred_element_type=F32
        )


def forward(gu_index, gu_count, down_index, down_count, got, gate, up, down):
    return pl.pallas_call(
        forward_kernel,
        out_shape=(
            jax.ShapeDtypeStruct((512, 6 * B), F32),
            jax.ShapeDtypeStruct((1024, 4 * B), BF16),
            jax.ShapeDtypeStruct((2 * B, 1024), BF16),
            jax.ShapeDtypeStruct((512, 1024), BF16),
            jax.ShapeDtypeStruct((512, 1024), BF16),
        ),
        in_specs=[SMEM] * 4 + [VMEM] * 4,
        out_specs=(VMEM,) * 5,
        name="forward",
    )(gu_index, gu_count, down_index, down_count, got, gate, up, down)


ORDER = (4, 3, 5, 2, 6, 1, 7)


def narrow_kernel(part, out, got, s_send, s_recv, g_send, g_recv):
    n = lax.axis_index("narrow")
    peers = {k: (n + k) % N for k in ORDER}
    greet("narrow", tuple(peers.values()))
    sums = [
        send("narrow", peers[k], part.at[peers[k]], got.at[k], s_send.at[k], s_recv.at[k])
        for k in ORDER
    ]
    total = part[n]
    for copy, k in zip(sums, ORDER):
        copy.wait_recv()
        total = total + got[k]
    gate, up, d_hidden = total[:, : 2 * B], total[:, 2 * B : 4 * B], total[:, 4 * B :]
    sig = jax.nn.sigmoid(gate)
    out[n, :, : 2 * B] = (gate * sig * up).astype(BF16)
    out[n, :, 2 * B : 4 * B] = (d_hidden * up * sig * (1.0 + gate * (1.0 - sig))).astype(BF16)
    out[n, :, 4 * B :] = (d_hidden * gate * sig).astype(BF16)
    shares = [
        send("narrow", peers[k], out.at[n], out.at[n], g_send.at[k], g_recv.at[k]) for k in ORDER
    ]
    for copy in shares:
        copy.wait_recv()
    for copy in sums + shares:
        copy.wait_send()


def narrow_step(part):
    return pl.pallas_call(
        narrow_kernel,
        out_shape=jax.ShapeDtypeStruct(part.shape, BF16),
        in_specs=[VMEM],
        out_specs=VMEM,
        scratch_shapes=[pltpu.VMEM(part.shape, F32)] + [pltpu.SemaphoreType.DMA((N,))] * 4,
        compiler_params=pltpu.CompilerParams(collective_id=1, has_side_effects=True),
        name="narrow_step",
    )(part)


def backward_kernel(
    gu_index, gu_count, down_index, down_count, units, xs, dys, wgu, dx, gate_g, up_g, down_g, dgu, dd
):
    grads = units[:, 2 * B :]

    @pl.loop(0, 4)
    def _(i):
        rows = pl.ds(pl.multiple_of(i * B, B), B)
        dx[rows, :] = lax.dot_general(
            units[rows, 2 * B :], wgu[...], (((1,), (1,)), ((), ())), preferred_element_type=F32
        )

    @pl.loop(0, 4)
    def _(i):
        cols = pl.ds(pl.multiple_of(i * 2 * B, 2 * B), 2 * B)
        dgu[cols, :] = lax.dot_general(
            xs[:, cols], grads, (((0,), (0,)), ((), ())), preferred_element_type=F32
        ).astype(BF16)

    dd[...] = lax.dot_general(
        units[:, : 2 * B], dys[...], (((0,), (0,)), ((), ())), preferred_element_type=F32
    ).astype(BF16)
    for s in range(gate_g.shape[0]):
        alive = s < gu_count[0]

        @pl.when(alive)
        def _():
            at = gu_index[s]
            row = pl.multiple_of((at // 2) * B, B)
            col = pl.multiple_of((at % 2) * B, B)
            gate_g[s] = dgu[pl.ds(row, B), pl.ds(col, B)]
            up_g[s] = dgu[pl.ds(row, B), pl.ds(2 * B + col, B)]

        @pl.when(jnp.logical_not(alive))
        def _():
            gate_g[s] = jnp.zeros((B, B), BF16)
            up_g[s] = jnp.zeros((B, B), BF16)

        d_alive = s < down_count[0]

        @pl.when(d_alive)
        def _():
            at = down_index[s]
            row = pl.multiple_of((at // 8) * B, B)
            col = pl.multiple_of((at % 8) * B, B)
            down_g[s] = dd[pl.ds(row, B), pl.ds(col, B)]

        @pl.when(jnp.logical_not(d_alive))
        def _():
            down_g[s] = jnp.zeros((B, B), BF16)


def backward(gu_index, gu_count, down_index, down_count, units, xs, dys, wgu, slots):
    grad = jax.ShapeDtypeStruct((slots, B, B), BF16)
    return pl.pallas_call(
        backward_kernel,
        out_shape=(jax.ShapeDtypeStruct((512, 1024), F32), grad, grad, grad),
        in_specs=[SMEM] * 4 + [VMEM] * 4,
        out_specs=(VMEM,) * 4,
        scratch_shapes=[pltpu.VMEM((1024, 4 * B), BF16), pltpu.VMEM((2 * B, 1024), BF16)],
        name="backward",
    )(gu_index, gu_count, down_index, down_count, units, xs, dys, wgu)


def scatter_kernel(part, out, held, run, last, c_send, c_recv, z_send, z_recv, y_sem):
    z, y, c = wide_place()
    right, left = wide_at(z + 1, y, c), wide_at(z - 1, y, c)
    across, partner = wide_at(z, 1 - y, c), wide_at(z, y, 1 - c)
    greet("wide", (right, left, across, partner))
    rows = (1 - y, y)

    order = []
    for s in range(8):
        order.append(8 - s)
        if s < 7:
            order.append(s - 7)
    order.append(0)
    cores = {}
    for k, off in enumerate(order):
        t = (z + off + Z) % Z
        cores[off] = send(
            "wide", partner, part.at[t, :, 1 - c], held.at[t], c_send.at[k], c_recv.at[k]
        )
    sent = list(cores.values())

    def mine(off, q):
        t = (z + off + Z) % Z
        return part[t, rows[q], c] + held[t, rows[q]]

    prev = {}
    for s in range(8):
        for q in (0, 1):
            for d in (0, 1):
                if s >= 8 - d:
                    continue
                off = 8 - s if d == 0 else s - 7
                if q == 0:
                    cores[off].wait_recv()
                if s == 0:
                    run[d, q, s] = mine(off, q)
                else:
                    prev[d, q].wait_recv()
                    run[d, q, s] = run[d, q, s] + mine(off, q)
                k = (d * 2 + q) * 8 + s
                prev[d, q] = send(
                    "wide",
                    right if d == 0 else left,
                    run.at[d, q, s],
                    run.at[d, q, s + 1],
                    z_send.at[k],
                    z_recv.at[k],
                )
                sent.append(prev[d, q])
    cores[0].wait_recv()

    def total(q):
        prev[1, q].wait_recv()
        left_sum = run[1, q, 7] + mine(0, q)
        prev[0, q].wait_recv()
        return left_sum + run[0, q, 8]

    last[0] = total(0)
    ycopy = send("wide", across, last.at[0], last.at[1], y_sem.at[0], y_sem.at[1])
    own = total(1)
    ycopy.wait_recv()
    out[...] = (own + last[1]).astype(BF16)
    for copy in sent + [ycopy]:
        copy.wait_send()


def scatter_wide(part):
    width = part.shape[-1]
    return pl.pallas_call(
        scatter_kernel,
        out_shape=jax.ShapeDtypeStruct((8, width), BF16),
        in_specs=[VMEM],
        out_specs=VMEM,
        scratch_shapes=[
            pltpu.VMEM((Z, 2, 8, width), F32),
            pltpu.VMEM((2, 2, 9, 8, width), F32),
            pltpu.VMEM((2, 8, width), F32),
            pltpu.SemaphoreType.DMA((Z,)),
            pltpu.SemaphoreType.DMA((Z,)),
            pltpu.SemaphoreType.DMA((32,)),
            pltpu.SemaphoreType.DMA((32,)),
            pltpu.SemaphoreType.DMA((2,)),
        ],
        compiler_params=pltpu.CompilerParams(collective_id=2, has_side_effects=True),
        name="scatter_wide",
    )(part)


def on_device(
    tokens, cotangent, gate_vals, up_vals, gu_index, gu_count, down_vals, down_index, down_count
):
    tables = (gu_index[0, 0], gu_count[0], down_index[0, 0], down_count[0])
    got = gather_wide(jnp.stack([tokens, cotangent]))
    part, wgu, _, xs, dys = forward(*tables, got, gate_vals[0, 0], up_vals[0, 0], down_vals[0, 0])
    units = narrow_step(part.reshape(N, 64, 6 * B)).reshape(512, 6 * B)
    dx, gate_g, up_g, down_g = backward(*tables, units, xs, dys, wgu, gate_vals.shape[2])
    d_tokens = scatter_wide(dx.reshape(Z, 2, 2, 8, dx.shape[-1]))
    return (d_tokens, gate_g[None, None], up_g[None, None], down_g[None, None])


def solution(mesh):
    in_specs = (
        P("wide", "narrow"),
        P("wide", "narrow"),
        P("narrow", "wide", None, None, None),
        P("narrow", "wide", None, None, None),
        P("narrow", "wide", None),
        P("narrow", "wide"),
        P("wide", "narrow", None, None, None),
        P("wide", "narrow", None),
        P("wide", "narrow"),
    )
    out_specs = (
        P("wide", "narrow"),
        P("narrow", "wide", None, None, None),
        P("narrow", "wide", None, None, None),
        P("wide", "narrow", None, None, None),
    )
    return jax.shard_map(
        on_device, mesh=mesh, in_specs=in_specs, out_specs=out_specs, check_vma=False
    )
```

```python
import jax
import jax.numpy as jnp
from jax import lax
from jax.experimental import pallas as pl
from jax.experimental.pallas import tpu as pltpu
from jax.sharding import PartitionSpec as P

MESH = pl.DeviceIdType.MESH
VMEM = pl.BlockSpec(memory_space=pltpu.VMEM)
SMEM = pl.BlockSpec(memory_space=pltpu.SMEM)
F32 = jnp.float32
BF16 = jnp.bfloat16

Z = 16
N = 8
B = 128


def wide_place():
    w = lax.axis_index("wide")
    return w // 4, (w // 2) % 2, w % 2


def wide_at(z, y, c):
    return ((z + Z) % Z * 2 + y) * 2 + c


def greet(peers):
    barrier = pltpu.get_barrier_semaphore()
    for axis, peer in peers:
        pl.semaphore_signal(barrier, inc=1, device_id={axis: peer}, device_id_type=MESH)
    pl.semaphore_wait(barrier, len(peers))


def send(axis, peer, src, dst, send_sem, recv_sem):
    copy = pltpu.make_async_remote_copy(
        src_ref=src,
        dst_ref=dst,
        send_sem=send_sem,
        recv_sem=recv_sem,
        device_id={axis: peer},
        device_id_type=MESH,
    )
    copy.start()
    return copy


def build_kernel(gu_index, gu_count, down_index, down_count, gate, up, down, wgu, wd):
    wgu[...] = jnp.zeros_like(wgu)
    wd[...] = jnp.zeros_like(wd)
    for s in range(gate.shape[0]):

        @pl.when(s < gu_count[0])
        def _():
            at = gu_index[s]
            row = pl.multiple_of((at // 2) * B, B)
            col = pl.multiple_of((at % 2) * B, B)
            wgu[pl.ds(row, B), pl.ds(col, B)] = gate[s]
            wgu[pl.ds(row, B), pl.ds(2 * B + col, B)] = up[s]

        @pl.when(s < down_count[0])
        def _():
            at = down_index[s]
            row = pl.multiple_of((at // 8) * B, B)
            col = pl.multiple_of((at % 8) * B, B)
            wd[pl.ds(row, B), pl.ds(col, B)] = down[s]


def build(tables, gate, up, down):
    return pl.pallas_call(
        build_kernel,
        out_shape=(
            jax.ShapeDtypeStruct((8 * B, 4 * B), BF16),
            jax.ShapeDtypeStruct((2 * B, 8 * B), BF16),
        ),
        in_specs=[SMEM] * 4 + [VMEM] * 3,
        out_specs=(VMEM,) * 2,
        name="build",
    )(*tables, gate, up, down)


ORDER = (4, 3, 5, 2, 6, 1, 7)


def front_kernel(
    mine,
    wgu,
    wd,
    units,
    xs,
    dys,
    got,
    part,
    sums,
    own_sem,
    y_sem,
    z_send,
    z_recv,
    c_send,
    c_recv,
    s_send,
    s_recv,
    g_send,
    g_recv,
):
    z, y, c = wide_place()
    n = lax.axis_index("narrow")
    right, left = wide_at(z + 1, y, c), wide_at(z - 1, y, c)
    across, partner = wide_at(z, 1 - y, c), wide_at(z, y, 1 - c)
    peers = {k: (n + k) % N for k in ORDER}
    greet([("wide", w) for w in (right, left, across, partner)] + [("narrow", p) for p in peers.values()])
    me = wide_at(z, y, c)
    rows = (y, 1 - y)
    ycopy = send("wide", across, mine, got.at[me], y_sem.at[0], y_sem.at[1])
    own = pltpu.make_async_copy(mine, got.at[me], own_sem)
    own.start()
    sent = [ycopy]
    cores = {}
    last = {}
    reduces = {}
    shares = []

    def ring(s):
        for q in (0, 1):
            for d in (0, 1):
                steps = 8 - d
                if s > steps + 1:
                    continue
                off = 1 - s if d == 0 else s - 1
                slot = wide_at(z + off, rows[q], c)
                src = got.at[slot]
                if s == 1:
                    if q == 0:
                        src = mine
                    elif d == 0:
                        ycopy.wait_recv()
                else:
                    last[d, q].wait_recv()
                if s <= steps:
                    k = (d * 2 + q) * 8 + s - 1
                    last[d, q] = send(
                        "wide",
                        right if d == 0 else left,
                        src,
                        got.at[slot],
                        z_send.at[k],
                        z_recv.at[k],
                    )
                    sent.append(last[d, q])
                if s > 1 or d == 0:
                    k = len(cores)
                    cores[off, q] = send(
                        "wide", partner, src, got.at[slot], c_send.at[k], c_recv.at[k]
                    )

    def chunk(k):
        offs = (-k, k) if k < 8 else (0, -8)
        for off in offs:
            for q in (0, 1):
                cores[off, q].wait_recv()
        slots = [wide_at(z + off, yy, cc) for off in offs for yy in (0, 1) for cc in (0, 1)]

        def rows_of(which):
            return jnp.concatenate([got[slot, which].astype(F32) for slot in slots], axis=0).astype(BF16)

        x = rows_of(0)
        xs[k - 1] = x
        gu = jnp.dot(x, wgu[...], preferred_element_type=F32)
        part[k - 1, :, :, : 4 * B] = gu.reshape(8, 8, 4 * B)
        dy = rows_of(1)
        dys[k - 1] = dy
        dh = lax.dot_general(dy, wd[...], (((1,), (1,)), ((), ())), preferred_element_type=F32)
        part[k - 1, :, :, 4 * B :] = dh.reshape(8, 8, 2 * B)
        for j in ORDER:
            reduces[k, j] = send(
                "narrow",
                peers[j],
                part.at[k - 1, peers[j]],
                sums.at[k - 1, j],
                s_send.at[k - 1, j],
                s_recv.at[k - 1, j],
            )

    def finish(k):
        total = part[k - 1, n]
        for j in ORDER:
            reduces[k, j].wait_recv()
            total = total + sums[k - 1, j]
        gate, up, d_hidden = total[:, : 2 * B], total[:, 2 * B : 4 * B], total[:, 4 * B :]
        sig = jax.nn.sigmoid(gate)
        units[k - 1, n, :, : 2 * B] = (gate * sig * up).astype(BF16)
        units[k - 1, n, :, 2 * B : 4 * B] = (
            d_hidden * up * sig * (1.0 + gate * (1.0 - sig))
        ).astype(BF16)
        units[k - 1, n, :, 4 * B :] = (d_hidden * gate * sig).astype(BF16)
        for j in ORDER:
            shares.append(
                send(
                    "narrow",
                    peers[j],
                    units.at[k - 1, n],
                    units.at[k - 1, n],
                    g_send.at[k - 1, j],
                    g_recv.at[k - 1, j],
                )
            )

    ring(1)
    own.wait()
    for s in range(2, 10):
        ring(s)
        chunk(s - 1)
        if s > 2:
            finish(s - 2)
    finish(8)
    for copy in shares:
        copy.wait_recv()
    for copy in sent + list(cores.values()) + list(reduces.values()) + shares:
        copy.wait_send()


def front(mine, wgu, wd):
    width = mine.shape[-1]
    sem = pltpu.SemaphoreType.DMA
    return pl.pallas_call(
        front_kernel,
        out_shape=(
            jax.ShapeDtypeStruct((8, N, 8, 6 * B), BF16),
            jax.ShapeDtypeStruct((8, 64, width), BF16),
            jax.ShapeDtypeStruct((8, 64, width), BF16),
        ),
        in_specs=[VMEM] * 3,
        out_specs=(VMEM,) * 3,
        scratch_shapes=[
            pltpu.VMEM((4 * Z,) + mine.shape, BF16),
            pltpu.VMEM((8, N, 8, 6 * B), F32),
            pltpu.VMEM((8, N, 8, 6 * B), F32),
            sem,
            sem((2,)),
            sem((32,)),
            sem((32,)),
            sem((32,)),
            sem((32,)),
            sem((8, N)),
            sem((8, N)),
            sem((8, N)),
            sem((8, N)),
        ],
        compiler_params=pltpu.CompilerParams(collective_id=0, has_side_effects=True),
        name="front",
    )(mine, wgu, wd)


def grads_kernel(
    gu_index, gu_count, down_index, down_count, units, xs, dys, gate_g, up_g, down_g, dgu, dd
):
    grads = units[:, 2 * B :]

    @pl.loop(0, 4)
    def _(i):
        cols = pl.ds(pl.multiple_of(i * 2 * B, 2 * B), 2 * B)
        dgu[cols, :] = lax.dot_general(
            xs[:, cols], grads, (((0,), (0,)), ((), ())), preferred_element_type=F32
        ).astype(BF16)

    dd[...] = lax.dot_general(
        units[:, : 2 * B], dys[...], (((0,), (0,)), ((), ())), preferred_element_type=F32
    ).astype(BF16)
    for s in range(gate_g.shape[0]):
        alive = s < gu_count[0]

        @pl.when(alive)
        def _():
            at = gu_index[s]
            row = pl.multiple_of((at // 2) * B, B)
            col = pl.multiple_of((at % 2) * B, B)
            gate_g[s] = dgu[pl.ds(row, B), pl.ds(col, B)]
            up_g[s] = dgu[pl.ds(row, B), pl.ds(2 * B + col, B)]

        @pl.when(jnp.logical_not(alive))
        def _():
            gate_g[s] = jnp.zeros((B, B), BF16)
            up_g[s] = jnp.zeros((B, B), BF16)

        d_alive = s < down_count[0]

        @pl.when(d_alive)
        def _():
            at = down_index[s]
            row = pl.multiple_of((at // 8) * B, B)
            col = pl.multiple_of((at % 8) * B, B)
            down_g[s] = dd[pl.ds(row, B), pl.ds(col, B)]

        @pl.when(jnp.logical_not(d_alive))
        def _():
            down_g[s] = jnp.zeros((B, B), BF16)


def block_grads(tables, units, xs, dys, slots):
    grad = jax.ShapeDtypeStruct((slots, B, B), BF16)
    return pl.pallas_call(
        grads_kernel,
        out_shape=(grad, grad, grad),
        in_specs=[SMEM] * 4 + [VMEM] * 3,
        out_specs=(VMEM,) * 3,
        scratch_shapes=[pltpu.VMEM((1024, 4 * B), BF16), pltpu.VMEM((2 * B, 1024), BF16)],
        name="block_grads",
    )(*tables, units, xs, dys)


def chunk_of(off):
    if off in (0, 8):
        return 7, (off == 8) * 1
    return abs(off) - 1, (off > 0) * 1


def scatter_kernel(units, wgu, out, part, held, run, last, c_send, c_recv, z_send, z_recv, y_sem):
    z, y, c = wide_place()
    right, left = wide_at(z + 1, y, c), wide_at(z - 1, y, c)
    across, partner = wide_at(z, 1 - y, c), wide_at(z, y, 1 - c)
    greet([("wide", w) for w in (right, left, across, partner)])
    rows = (1 - y, y)
    cores = {}

    def terms(s):
        offs = (8 - s, s - 7)
        places = [chunk_of(off) for off in offs]
        picked = jnp.concatenate(
            [units[k, 4 * 8 * j : 4 * 8 * (j + 1), 2 * B :] for k, j in places], axis=0
        )
        dx = lax.dot_general(
            picked, wgu[...], (((1,), (1,)), ((), ())), preferred_element_type=F32
        ).reshape(2, 2, 2, 8, -1)
        for i, (k, j) in enumerate(places):
            part[k, j] = dx[i]
            a = 2 * s + i
            cores[offs[i]] = send(
                "wide", partner, part.at[k, j, :, 1 - c], held.at[k, j], c_send.at[a], c_recv.at[a]
            )

    def mine(off, q):
        k, j = chunk_of(off)
        return part[k, j, rows[q], c] + held[k, j, rows[q]]

    prev = {}
    sent = []
    terms(0)
    terms(1)
    for s in range(8):
        for q in (0, 1):
            for d in (0, 1):
                if s >= 8 - d:
                    continue
                off = 8 - s if d == 0 else s - 7
                if q == 0:
                    cores[off].wait_recv()
                if s == 0:
                    run[d, q, s] = mine(off, q)
                else:
                    prev[d, q].wait_recv()
                    run[d, q, s] = run[d, q, s] + mine(off, q)
                k = (d * 2 + q) * 8 + s
                prev[d, q] = send(
                    "wide",
                    right if d == 0 else left,
                    run.at[d, q, s],
                    run.at[d, q, s + 1],
                    z_send.at[k],
                    z_recv.at[k],
                )
                sent.append(prev[d, q])
        if s + 2 < 8:
            terms(s + 2)
    cores[0].wait_recv()

    def total(q):
        prev[1, q].wait_recv()
        left_sum = run[1, q, 7] + mine(0, q)
        prev[0, q].wait_recv()
        return left_sum + run[0, q, 8]

    last[0] = total(0)
    ycopy = send("wide", across, last.at[0], last.at[1], y_sem.at[0], y_sem.at[1])
    own = total(1)
    ycopy.wait_recv()
    out[...] = (own + last[1]).astype(BF16)
    for copy in sent + list(cores.values()) + [ycopy]:
        copy.wait_send()


def scatter_wide(units, wgu):
    width = wgu.shape[0]
    sem = pltpu.SemaphoreType.DMA
    return pl.pallas_call(
        scatter_kernel,
        out_shape=jax.ShapeDtypeStruct((8, width), BF16),
        in_specs=[VMEM] * 2,
        out_specs=VMEM,
        scratch_shapes=[
            pltpu.VMEM((8, 2, 2, 2, 8, width), F32),
            pltpu.VMEM((8, 2, 2, 8, width), F32),
            pltpu.VMEM((2, 2, 9, 8, width), F32),
            pltpu.VMEM((2, 8, width), F32),
            sem((Z,)),
            sem((Z,)),
            sem((32,)),
            sem((32,)),
            sem((2,)),
        ],
        compiler_params=pltpu.CompilerParams(collective_id=2, has_side_effects=True),
        name="scatter_wide",
    )(units, wgu)


def on_device(
    tokens, cotangent, gate_vals, up_vals, gu_index, gu_count, down_vals, down_index, down_count
):
    tables = (gu_index[0, 0], gu_count[0], down_index[0, 0], down_count[0])
    wgu, wd = build(tables, gate_vals[0, 0], up_vals[0, 0], down_vals[0, 0])
    units, xs, dys = front(jnp.stack([tokens, cotangent]), wgu, wd)
    d_tokens = scatter_wide(units.reshape(8, 64, -1), wgu)
    gate_g, up_g, down_g = block_grads(
        tables, *(v.reshape(512, -1) for v in (units, xs, dys)), gate_vals.shape[2]
    )
    return (d_tokens, gate_g[None, None], up_g[None, None], down_g[None, None])


def solution(mesh):
    in_specs = (
        P("wide", "narrow"),
        P("wide", "narrow"),
        P("narrow", "wide", None, None, None),
        P("narrow", "wide", None, None, None),
        P("narrow", "wide", None),
        P("narrow", "wide"),
        P("wide", "narrow", None, None, None),
        P("wide", "narrow", None),
        P("wide", "narrow"),
    )
    out_specs = (
        P("wide", "narrow"),
        P("narrow", "wide", None, None, None),
        P("narrow", "wide", None, None, None),
        P("wide", "narrow", None, None, None),
    )
    return jax.shard_map(
        on_device, mesh=mesh, in_specs=in_specs, out_specs=out_specs, check_vma=False
    )
```

```python
import jax
import jax.numpy as jnp
from jax import lax
from jax.experimental import pallas as pl
from jax.experimental.pallas import tpu as pltpu
from jax.sharding import PartitionSpec as P

MESH = pl.DeviceIdType.MESH
VMEM = pl.BlockSpec(memory_space=pltpu.VMEM)
SMEM = pl.BlockSpec(memory_space=pltpu.SMEM)
F32 = jnp.float32
BF16 = jnp.bfloat16

Z = 16
N = 8
B = 128


def wide_place():
    w = lax.axis_index("wide")
    return w // 4, (w // 2) % 2, w % 2


def wide_at(z, y, c):
    return ((z + Z) % Z * 2 + y) * 2 + c


def greet(peers):
    barrier = pltpu.get_barrier_semaphore()
    for axis, peer in peers:
        pl.semaphore_signal(barrier, inc=1, device_id={axis: peer}, device_id_type=MESH)
    pl.semaphore_wait(barrier, len(peers))


def send(axis, peer, src, dst, send_sem, recv_sem):
    copy = pltpu.make_async_remote_copy(
        src_ref=src,
        dst_ref=dst,
        send_sem=send_sem,
        recv_sem=recv_sem,
        device_id={axis: peer},
        device_id_type=MESH,
    )
    copy.start()
    return copy


def tables_kernel(gu_index, gu_count, down_index, down_count, out):
    for base, index, count in ((0, gu_index, gu_count), (4, down_index, down_count)):
        live = count[0, 0]
        for block in range(16):
            out[base + 2, block] = 0
            out[base + 3, block] = 0
        for s in range(index.shape[-1]):
            at = index[0, 0, s]
            out[base, s] = at
            out[base + 1, s] = jnp.where(s < live, 1, 0)

            @pl.when(s < live)
            def _():
                out[base + 2, at] = s
                out[base + 3, at] = 1


def tables_of(*args):
    return pl.pallas_call(
        tables_kernel,
        out_shape=jax.ShapeDtypeStruct((8, 16), jnp.int32),
        in_specs=[SMEM] * 4,
        out_specs=SMEM,
        name="tables",
    )(*args)


def only_if(flag, value):
    return jnp.where(jnp.full(value.shape, flag) > 0, value.astype(F32), 0.0).astype(BF16)


ORDER = (4, 3, 5, 2, 6, 1, 7)


def front_kernel(
    tables,
    tokens,
    cotangent,
    gate,
    up,
    down,
    units,
    wgu,
    xs,
    dys,
    wd,
    got,
    part,
    sums,
    own_sem,
    y_sem,
    z_send,
    z_recv,
    c_send,
    c_recv,
    s_send,
    s_recv,
    g_send,
    g_recv,
):
    z, y, c = wide_place()
    n = lax.axis_index("narrow")
    right, left = wide_at(z + 1, y, c), wide_at(z - 1, y, c)
    across, partner = wide_at(z, 1 - y, c), wide_at(z, y, 1 - c)
    peers = {k: (n + k) % N for k in ORDER}
    me = wide_at(z, y, c)
    owns = [
        pltpu.make_async_copy(ref, got.at[me, i], own_sem.at[i])
        for i, ref in enumerate((tokens, cotangent))
    ]
    for copy in owns:
        copy.start()
    greet([("wide", w) for w in (right, left, across, partner)] + [("narrow", p) for p in peers.values()])
    for copy in owns:
        copy.wait()
    mine = got.at[me]
    rows = (y, 1 - y)
    ycopy = send("wide", across, mine, got.at[me], y_sem.at[0], y_sem.at[1])
    sent = [ycopy]
    cores = {}
    last = {}
    reduces = {}
    shares = []

    def ring(s, q):
        for d in (0, 1):
            steps = 8 - d
            if s > steps + 1:
                continue
            off = 1 - s if d == 0 else s - 1
            slot = wide_at(z + off, rows[q], c)
            src = got.at[slot]
            if s > 1:
                last[d, q].wait_recv()
            elif q == 1 and d == 0:
                ycopy.wait_recv()
            if s <= steps:
                k = (d * 2 + q) * 8 + s - 1
                last[d, q] = send(
                    "wide", right if d == 0 else left, src, src, z_send.at[k], z_recv.at[k]
                )
                sent.append(last[d, q])
            if s > 1 or d == 0:
                k = len(cores)
                cores[off, q] = send("wide", partner, src, src, c_send.at[k], c_recv.at[k])

    def chunk(k):
        offs = (-k, k) if k < 8 else (0, -8)
        for off in offs:
            for q in (0, 1):
                cores[off, q].wait_recv()
        slots = [wide_at(z + off, yy, cc) for off in offs for yy in (0, 1) for cc in (0, 1)]

        def rows_of(which):
            return jnp.concatenate([got[slot, which].astype(F32) for slot in slots], axis=0).astype(BF16)

        x = rows_of(0)
        xs[k - 1] = x
        gu = jnp.dot(x, wgu[...], preferred_element_type=F32)
        part[k - 1, :, :, : 4 * B] = gu.reshape(8, 8, 4 * B)
        dy = rows_of(1)
        dys[k - 1] = dy
        dh = lax.dot_general(dy, wd[...], (((1,), (1,)), ((), ())), preferred_element_type=F32)
        part[k - 1, :, :, 4 * B :] = dh.reshape(8, 8, 2 * B)
        for j in ORDER:
            reduces[k, j] = send(
                "narrow",
                peers[j],
                part.at[k - 1, peers[j]],
                sums.at[k - 1, j],
                s_send.at[k - 1, j],
                s_recv.at[k - 1, j],
            )

    def finish(k):
        total = part[k - 1, n]
        for j in ORDER:
            reduces[k, j].wait_recv()
            total = total + sums[k - 1, j]
        gate, up, d_hidden = total[:, : 2 * B], total[:, 2 * B : 4 * B], total[:, 4 * B :]
        sig = jax.nn.sigmoid(gate)
        units[k - 1, n, :, : 2 * B] = (gate * sig * up).astype(BF16)
        units[k - 1, n, :, 2 * B : 4 * B] = (
            d_hidden * up * sig * (1.0 + gate * (1.0 - sig))
        ).astype(BF16)
        units[k - 1, n, :, 4 * B :] = (d_hidden * gate * sig).astype(BF16)
        for j in ORDER:
            shares.append(
                send(
                    "narrow",
                    peers[j],
                    units.at[k - 1, n],
                    units.at[k - 1, n],
                    g_send.at[k - 1, j],
                    g_recv.at[k - 1, j],
                )
            )

    def place(table, sources, target, width):
        for block in range(16):
            row, col = block // width * B, block % width * B
            slot, flag = tables[table + 2, block], tables[table + 3, block]
            for i, source in enumerate(sources):
                at = 2 * B * i + col
                target[row : row + B, at : at + B] = only_if(flag, source[slot])

    for i in range(1, 12):
        if i <= 9:
            ring(i, 0)
        if i == 1:
            place(0, (gate, up), wgu, 2)
            place(4, (down,), wd, 8)
        elif i <= 10:
            ring(i - 1, 1)
        if i > 3:
            chunk(i - 3)
        if i > 4:
            finish(i - 4)
    finish(8)
    for copy in shares:
        copy.wait_recv()
    for copy in sent + list(cores.values()) + list(reduces.values()) + shares:
        copy.wait_send()


def front(tables, tokens, cotangent, gate, up, down):
    width = tokens.shape[-1]
    sem = pltpu.SemaphoreType.DMA
    return pl.pallas_call(
        front_kernel,
        out_shape=(
            jax.ShapeDtypeStruct((8, N, 8, 6 * B), BF16),
            jax.ShapeDtypeStruct((8 * B, 4 * B), BF16),
            jax.ShapeDtypeStruct((8, 64, width), BF16),
            jax.ShapeDtypeStruct((8, 64, width), BF16),
        ),
        in_specs=[SMEM] + [VMEM] * 5,
        out_specs=(VMEM,) * 4,
        scratch_shapes=[
            pltpu.VMEM((2 * B, 8 * B), BF16),
            pltpu.VMEM((4 * Z, 2, 8, width), BF16),
            pltpu.VMEM((8, N, 8, 6 * B), F32),
            pltpu.VMEM((8, N, 8, 6 * B), F32),
            sem((2,)),
            sem((2,)),
            sem((32,)),
            sem((32,)),
            sem((32,)),
            sem((32,)),
            sem((8, N)),
            sem((8, N)),
            sem((8, N)),
            sem((8, N)),
        ],
        compiler_params=pltpu.CompilerParams(collective_id=0, has_side_effects=True),
        name="front",
    )(tables, tokens, cotangent, gate, up, down)


def chunk_of(off):
    if off in (0, 8):
        return 7, (off == 8) * 1
    return abs(off) - 1, (off > 0) * 1


def back_kernel(
    tables,
    units,
    wgu,
    xs,
    dys,
    out,
    gate_g,
    up_g,
    down_g,
    dgu,
    dd,
    part,
    held,
    run,
    last,
    c_send,
    c_recv,
    z_send,
    z_recv,
    y_sem,
):
    z, y, c = wide_place()
    right, left = wide_at(z + 1, y, c), wide_at(z - 1, y, c)
    across, partner = wide_at(z, 1 - y, c), wide_at(z, y, 1 - c)
    greet([("wide", w) for w in (right, left, across, partner)])
    rows = (1 - y, y)
    cores = {}

    def terms(s):
        offs = (8 - s, s - 7)
        places = [chunk_of(off) for off in offs]
        picked = jnp.concatenate(
            [units[64 * k + 32 * j : 64 * k + 32 * (j + 1), 2 * B :] for k, j in places], axis=0
        )
        dx = lax.dot_general(
            picked, wgu[...], (((1,), (1,)), ((), ())), preferred_element_type=F32
        ).reshape(2, 2, 2, 8, -1)
        for i, (k, j) in enumerate(places):
            part[k, j] = dx[i]
            a = 2 * s + i
            cores[offs[i]] = send(
                "wide", partner, part.at[k, j, :, 1 - c], held.at[k, j], c_send.at[a], c_recv.at[a]
            )

    def mine(off, q):
        k, j = chunk_of(off)
        return part[k, j, rows[q], c] + held[k, j, rows[q]]

    def across_tokens(a, b):
        return lax.dot_general(
            a, b, (((0,), (0,)), ((), ())), preferred_element_type=F32
        ).astype(BF16)

    def gradients(s):
        if s < 4:
            dense = across_tokens(xs[:, 2 * B * s : 2 * B * (s + 1)], units[:, 2 * B :])
            for row in (0, 1):
                for i in (0, 1):
                    for col in (0, 1):
                        at = B * (2 * i + col)
                        dgu[i, 2 * (2 * s + row) + col] = dense[row * B : (row + 1) * B, at : at + B]
        elif s < 6:
            half = s - 4
            dense = across_tokens(units[:, : 2 * B], dys[:, 4 * B * half : 4 * B * (half + 1)])
            for row in (0, 1):
                for col in range(4):
                    dd[8 * row + 4 * half + col] = dense[row * B : (row + 1) * B, col * B : (col + 1) * B]
        elif s == 6:
            for k in range(gate_g.shape[0]):
                gate_g[k] = only_if(tables[1, k], dgu[0, tables[0, k]])
                up_g[k] = only_if(tables[1, k], dgu[1, tables[0, k]])
        else:
            for k in range(down_g.shape[0]):
                down_g[k] = only_if(tables[5, k], dd[tables[4, k]])

    prev = {}
    sent = []
    terms(0)
    terms(1)

    def step(s, q):
        for d in (0, 1):
            if s >= 8 - d:
                continue
            off = 8 - s if d == 0 else s - 7
            if q == 0:
                cores[off].wait_recv()
            if s == 0:
                run[d, q, s] = mine(off, q)
            else:
                prev[d, q].wait_recv()
                run[d, q, s] = run[d, q, s] + mine(off, q)
            k = (d * 2 + q) * 8 + s
            prev[d, q] = send(
                "wide",
                right if d == 0 else left,
                run.at[d, q, s],
                run.at[d, q, s + 1],
                z_send.at[k],
                z_recv.at[k],
            )
            sent.append(prev[d, q])

    for i in range(9):
        if i < 8:
            step(i, 0)
        if i > 0:
            step(i - 1, 1)
        if i + 2 < 8:
            terms(i + 2)
        if i < 8:
            gradients(i)
    cores[0].wait_recv()

    def total(q):
        prev[1, q].wait_recv()
        left_sum = run[1, q, 7] + mine(0, q)
        prev[0, q].wait_recv()
        return left_sum + run[0, q, 8]

    last[0] = total(0)
    ycopy = send("wide", across, last.at[0], last.at[1], y_sem.at[0], y_sem.at[1])
    own = total(1)
    ycopy.wait_recv()
    out[...] = (own + last[1]).astype(BF16)
    for copy in sent + list(cores.values()) + [ycopy]:
        copy.wait_send()


def back(tables, units, wgu, xs, dys, slots):
    width = wgu.shape[0]
    sem = pltpu.SemaphoreType.DMA
    grad = jax.ShapeDtypeStruct((slots, B, B), BF16)
    return pl.pallas_call(
        back_kernel,
        out_shape=(jax.ShapeDtypeStruct((8, width), BF16), grad, grad, grad),
        in_specs=[SMEM] + [VMEM] * 4,
        out_specs=(VMEM,) * 4,
        scratch_shapes=[
            pltpu.VMEM((2, 16, B, B), BF16),
            pltpu.VMEM((16, B, B), BF16),
            pltpu.VMEM((8, 2, 2, 2, 8, width), F32),
            pltpu.VMEM((8, 2, 2, 8, width), F32),
            pltpu.VMEM((2, 2, 9, 8, width), F32),
            pltpu.VMEM((2, 8, width), F32),
            sem((Z,)),
            sem((Z,)),
            sem((32,)),
            sem((32,)),
            sem((2,)),
        ],
        compiler_params=pltpu.CompilerParams(collective_id=2, has_side_effects=True),
        name="back",
    )(tables, units, wgu, xs, dys)


def on_device(
    tokens, cotangent, gate_vals, up_vals, gu_index, gu_count, down_vals, down_index, down_count
):
    tables = tables_of(gu_index, gu_count, down_index, down_count)
    units, wgu, xs, dys = front(
        tables, tokens, cotangent, gate_vals[0, 0], up_vals[0, 0], down_vals[0, 0]
    )
    d_tokens, gate_g, up_g, down_g = back(
        tables, units.reshape(512, -1), wgu, xs.reshape(512, -1), dys.reshape(512, -1), gate_vals.shape[2]
    )
    return (d_tokens, gate_g[None, None], up_g[None, None], down_g[None, None])


def solution(mesh):
    in_specs = (
        P("wide", "narrow"),
        P("wide", "narrow"),
        P("narrow", "wide", None, None, None),
        P("narrow", "wide", None, None, None),
        P("narrow", "wide", None),
        P("narrow", "wide"),
        P("wide", "narrow", None, None, None),
        P("wide", "narrow", None),
        P("wide", "narrow"),
    )
    out_specs = (
        P("wide", "narrow"),
        P("narrow", "wide", None, None, None),
        P("narrow", "wide", None, None, None),
        P("wide", "narrow", None, None, None),
    )
    return jax.shard_map(
        on_device, mesh=mesh, in_specs=in_specs, out_specs=out_specs, check_vma=False
    )
```

```python
import jax
import jax.numpy as jnp
from jax import lax
from jax.experimental import pallas as pl
from jax.experimental.pallas import tpu as pltpu
from jax.sharding import PartitionSpec as P

MESH = pl.DeviceIdType.MESH
VMEM = pl.BlockSpec(memory_space=pltpu.VMEM)
SMEM = pl.BlockSpec(memory_space=pltpu.SMEM)
F32 = jnp.float32
BF16 = jnp.bfloat16

Z = 16
N = 8
B = 128


def wide_place():
    w = lax.axis_index("wide")
    return w // 4, (w // 2) % 2, w % 2


def wide_at(z, y, c):
    return ((z + Z) % Z * 2 + y) * 2 + c


def greet(peers):
    barrier = pltpu.get_barrier_semaphore()
    for axis, peer in peers:
        pl.semaphore_signal(barrier, inc=1, device_id={axis: peer}, device_id_type=MESH)
    pl.semaphore_wait(barrier, len(peers))


def send(axis, peer, src, dst, send_sem, recv_sem):
    copy = pltpu.make_async_remote_copy(
        src_ref=src,
        dst_ref=dst,
        send_sem=send_sem,
        recv_sem=recv_sem,
        device_id={axis: peer},
        device_id_type=MESH,
    )
    copy.start()
    return copy


def tables_kernel(gu_index, gu_count, down_index, down_count, out):
    for base, index, count in ((0, gu_index, gu_count), (4, down_index, down_count)):
        live = count[0, 0]
        for block in range(16):
            out[base + 2, block] = 0
            out[base + 3, block] = 0
        for s in range(index.shape[-1]):
            at = index[0, 0, s]
            out[base, s] = at
            out[base + 1, s] = jnp.where(s < live, 1, 0)

            @pl.when(s < live)
            def _():
                out[base + 2, at] = s
                out[base + 3, at] = 1


def tables_of(*args):
    return pl.pallas_call(
        tables_kernel,
        out_shape=jax.ShapeDtypeStruct((8, 16), jnp.int32),
        in_specs=[SMEM] * 4,
        out_specs=SMEM,
        name="tables",
    )(*args)


def only_if(flag, value):
    return jnp.where(jnp.full(value.shape, flag) > 0, value.astype(F32), 0.0).astype(BF16)


ORDER = (4, 3, 5, 2, 6, 1, 7)


def layer_kernel(
    tables,
    tokens,
    cotangent,
    gate,
    up,
    down,
    out,
    dgu,
    dd,
    units,
    flat,
    wgu,
    xs,
    dys,
    wd,
    got,
    part,
    sums,
    own_sem,
    y_sem,
    z_send,
    z_recv,
    c_send,
    c_recv,
    s_send,
    s_recv,
    g_send,
    g_recv,
    *back_refs,
):
    z, y, c = wide_place()
    n = lax.axis_index("narrow")
    right, left = wide_at(z + 1, y, c), wide_at(z - 1, y, c)
    across, partner = wide_at(z, 1 - y, c), wide_at(z, y, 1 - c)
    peers = {k: (n + k) % N for k in ORDER}
    me = wide_at(z, y, c)
    owns = [
        pltpu.make_async_copy(ref, got.at[me, i], own_sem.at[i])
        for i, ref in enumerate((tokens, cotangent))
    ]
    for copy in owns:
        copy.start()
    greet([("wide", w) for w in (right, left, across, partner)] + [("narrow", p) for p in peers.values()])
    for copy in owns:
        copy.wait()
    mine = got.at[me]
    rows = (y, 1 - y)
    ycopy = send("wide", across, mine, got.at[me], y_sem.at[0], y_sem.at[1])
    sent = [ycopy]
    cores = {}
    last = {}
    reduces = {}
    shares = {}

    def ring(s, q):
        for d in (0, 1):
            steps = 8 - d
            if s > steps + 1:
                continue
            off = 1 - s if d == 0 else s - 1
            slot = wide_at(z + off, rows[q], c)
            src = got.at[slot]
            if s > 1:
                last[d, q].wait_recv()
            elif q == 1 and d == 0:
                ycopy.wait_recv()
            if s <= steps:
                k = (d * 2 + q) * 8 + s - 1
                last[d, q] = send(
                    "wide", right if d == 0 else left, src, src, z_send.at[k], z_recv.at[k]
                )
                sent.append(last[d, q])
            if s > 1 or d == 0:
                k = len(cores)
                cores[off, q] = send("wide", partner, src, src, c_send.at[k], c_recv.at[k])

    def chunk(k):
        offs = (-k, k) if k < 8 else (0, -8)
        for off in offs:
            for q in (0, 1):
                cores[off, q].wait_recv()
        slots = [wide_at(z + off, yy, cc) for off in offs for yy in (0, 1) for cc in (0, 1)]

        def rows_of(which):
            return jnp.concatenate([got[slot, which].astype(F32) for slot in slots], axis=0).astype(BF16)

        x = rows_of(0)
        xs[64 * (k - 1) : 64 * k, :] = x
        gu = jnp.dot(x, wgu[...], preferred_element_type=F32)
        part[k - 1, :, :, : 4 * B] = gu.reshape(8, 8, 4 * B)
        dy = rows_of(1)
        dys[64 * (k - 1) : 64 * k, :] = dy
        dh = lax.dot_general(dy, wd[...], (((1,), (1,)), ((), ())), preferred_element_type=F32)
        part[k - 1, :, :, 4 * B :] = dh.reshape(8, 8, 2 * B)
        for j in ORDER:
            reduces[k, j] = send(
                "narrow",
                peers[j],
                part.at[k - 1, peers[j]],
                sums.at[k - 1, j],
                s_send.at[k - 1, j],
                s_recv.at[k - 1, j],
            )

    def finish(k):
        total = part[k - 1, n]
        for j in ORDER:
            reduces[k, j].wait_recv()
            total = total + sums[k - 1, j]
        gate, up, d_hidden = total[:, : 2 * B], total[:, 2 * B : 4 * B], total[:, 4 * B :]
        sig = jax.nn.sigmoid(gate)
        units[k - 1, n, :, : 2 * B] = (gate * sig * up).astype(BF16)
        units[k - 1, n, :, 2 * B : 4 * B] = (
            d_hidden * up * sig * (1.0 + gate * (1.0 - sig))
        ).astype(BF16)
        units[k - 1, n, :, 4 * B :] = (d_hidden * gate * sig).astype(BF16)
        for j in ORDER:
            shares[k, j] = send(
                "narrow",
                peers[j],
                units.at[k - 1, n],
                units.at[k - 1, n],
                g_send.at[k - 1, j],
                g_recv.at[k - 1, j],
            )

    def settle(k):
        for j in ORDER:
            shares[k, j].wait_recv()
        flat[64 * (k - 1) : 64 * k, :] = units[k - 1].astype(F32).reshape(64, -1).astype(BF16)

    def place(table, sources, target, width):
        for block in range(16):
            row, col = block // width * B, block % width * B
            slot, flag = tables[table + 2, block], tables[table + 3, block]
            for i, source in enumerate(sources):
                at = 2 * B * i + col
                target[row : row + B, at : at + B] = only_if(flag, source[slot])

    for i in range(1, 12):
        if i <= 9:
            ring(i, 0)
        if i == 1:
            place(0, (gate, up), wgu, 2)
            place(4, (down,), wd, 8)
        elif i <= 10:
            ring(i - 1, 1)
        if i > 3:
            chunk(i - 3)
        if i > 4:
            finish(i - 4)
        if i > 5:
            settle(i - 5)
    finish(8)
    settle(7)
    settle(8)
    back(flat, wgu, xs, dys, out, dgu, dd, *back_refs)
    for group in (cores, reduces, shares):
        sent.extend(group.values())
    for copy in sent:
        copy.wait_send()


def chunk_of(off):
    if off in (0, 8):
        return 7, (off == 8) * 1
    return abs(off) - 1, (off > 0) * 1


def back(
    units, wgu, xs, dys, out, dgu, dd, part, held, run, last, c_send, c_recv, z_send, z_recv, y_sem
):
    z, y, c = wide_place()
    right, left = wide_at(z + 1, y, c), wide_at(z - 1, y, c)
    across, partner = wide_at(z, 1 - y, c), wide_at(z, y, 1 - c)
    rows = (1 - y, y)
    cores = {}

    def terms(s):
        offs = (8 - s, s - 7)
        places = [chunk_of(off) for off in offs]
        picked = jnp.concatenate(
            [units[64 * k + 32 * j : 64 * k + 32 * (j + 1), 2 * B :] for k, j in places], axis=0
        )
        dx = lax.dot_general(
            picked, wgu[...], (((1,), (1,)), ((), ())), preferred_element_type=F32
        ).reshape(2, 2, 2, 8, -1)
        for i, (k, j) in enumerate(places):
            part[k, j] = dx[i]
            a = 2 * s + i
            cores[offs[i]] = send(
                "wide", partner, part.at[k, j, :, 1 - c], held.at[k, j], c_send.at[a], c_recv.at[a]
            )

    def mine(off, q):
        k, j = chunk_of(off)
        return part[k, j, rows[q], c] + held[k, j, rows[q]]

    def across_tokens(a, b):
        return lax.dot_general(
            a, b, (((0,), (0,)), ((), ())), preferred_element_type=F32
        ).astype(BF16)

    def gradients(s):
        if s < 4:
            dense = across_tokens(xs[:, 2 * B * s : 2 * B * (s + 1)], units[:, 2 * B :])
            for row in (0, 1):
                for i in (0, 1):
                    for col in (0, 1):
                        at = B * (2 * i + col)
                        dgu[i, 2 * (2 * s + row) + col] = dense[row * B : (row + 1) * B, at : at + B]
        elif s < 6:
            half = s - 4
            dense = across_tokens(units[:, : 2 * B], dys[:, 4 * B * half : 4 * B * (half + 1)])
            for row in (0, 1):
                for col in range(4):
                    dd[8 * row + 4 * half + col] = dense[row * B : (row + 1) * B, col * B : (col + 1) * B]

    prev = {}
    sent = []
    terms(0)
    terms(1)

    def step(s, q):
        for d in (0, 1):
            if s >= 8 - d:
                continue
            off = 8 - s if d == 0 else s - 7
            if q == 0:
                cores[off].wait_recv()
            if s == 0:
                run[d, q, s] = mine(off, q)
            else:
                prev[d, q].wait_recv()
                run[d, q, s] = run[d, q, s] + mine(off, q)
            k = (d * 2 + q) * 8 + s
            prev[d, q] = send(
                "wide",
                right if d == 0 else left,
                run.at[d, q, s],
                run.at[d, q, s + 1],
                z_send.at[k],
                z_recv.at[k],
            )
            sent.append(prev[d, q])

    for i in range(9):
        if i < 8:
            step(i, 0)
        if i > 0:
            step(i - 1, 1)
        if i + 2 < 8:
            terms(i + 2)
        if i < 8:
            gradients(i)
    cores[0].wait_recv()

    def total(q):
        prev[1, q].wait_recv()
        left_sum = run[1, q, 7] + mine(0, q)
        prev[0, q].wait_recv()
        return left_sum + run[0, q, 8]

    last[0] = total(0)
    ycopy = send("wide", across, last.at[0], last.at[1], y_sem.at[0], y_sem.at[1])
    own = total(1)
    ycopy.wait_recv()
    out[...] = (own + last[1]).astype(BF16)
    for copy in sent + list(cores.values()) + [ycopy]:
        copy.wait_send()


def layer(tables, tokens, cotangent, gate, up, down):
    width = tokens.shape[-1]
    sem = pltpu.SemaphoreType.DMA
    return pl.pallas_call(
        layer_kernel,
        out_shape=(
            jax.ShapeDtypeStruct((8, width), BF16),
            jax.ShapeDtypeStruct((2, 16, B, B), BF16),
            jax.ShapeDtypeStruct((16, B, B), BF16),
        ),
        in_specs=[SMEM] + [VMEM] * 5,
        out_specs=(VMEM,) * 3,
        scratch_shapes=[
            pltpu.VMEM((8, N, 8, 6 * B), BF16),
            pltpu.VMEM((512, 6 * B), BF16),
            pltpu.VMEM((8 * B, 4 * B), BF16),
            pltpu.VMEM((512, width), BF16),
            pltpu.VMEM((512, width), BF16),
            pltpu.VMEM((2 * B, 8 * B), BF16),
            pltpu.VMEM((4 * Z, 2, 8, width), BF16),
            pltpu.VMEM((8, N, 8, 6 * B), F32),
            pltpu.VMEM((8, N, 8, 6 * B), F32),
            sem((2,)),
            sem((2,)),
            sem((32,)),
            sem((32,)),
            sem((32,)),
            sem((32,)),
            sem((8, N)),
            sem((8, N)),
            sem((8, N)),
            sem((8, N)),
            pltpu.VMEM((8, 2, 2, 2, 8, width), F32),
            pltpu.VMEM((8, 2, 2, 8, width), F32),
            pltpu.VMEM((2, 2, 9, 8, width), F32),
            pltpu.VMEM((2, 8, width), F32),
            sem((Z,)),
            sem((Z,)),
            sem((32,)),
            sem((32,)),
            sem((2,)),
        ],
        compiler_params=pltpu.CompilerParams(collective_id=0, has_side_effects=True),
        name="layer",
    )(tables, tokens, cotangent, gate, up, down)


def pick_kernel(gu_index, gu_count, down_index, down_count, mine, dgu, dd, out, gate_g, up_g, down_g):
    out[...] = mine[...]
    for s in range(gate_g.shape[0]):
        alive = s < gu_count[0, 0]

        @pl.when(alive)
        def _():
            at = gu_index[0, 0, s]
            gate_g[s] = dgu[0, at]
            up_g[s] = dgu[1, at]

        @pl.when(jnp.logical_not(alive))
        def _():
            gate_g[s] = jnp.zeros((B, B), BF16)
            up_g[s] = jnp.zeros((B, B), BF16)

        d_alive = s < down_count[0, 0]

        @pl.when(d_alive)
        def _():
            down_g[s] = dd[down_index[0, 0, s]]

        @pl.when(jnp.logical_not(d_alive))
        def _():
            down_g[s] = jnp.zeros((B, B), BF16)


def pick(places, mine, dgu, dd, slots):
    grad = jax.ShapeDtypeStruct((slots, B, B), BF16)
    return pl.pallas_call(
        pick_kernel,
        out_shape=(jax.ShapeDtypeStruct(mine.shape, BF16), grad, grad, grad),
        in_specs=[SMEM] * 4 + [VMEM] * 3,
        out_specs=(VMEM,) * 4,
        name="pick",
    )(*places, mine, dgu, dd)


def on_device(
    tokens, cotangent, gate_vals, up_vals, gu_index, gu_count, down_vals, down_index, down_count
):
    places = (gu_index, gu_count, down_index, down_count)
    mine, dgu, dd = layer(
        tables_of(*places), tokens, cotangent, gate_vals[0, 0], up_vals[0, 0], down_vals[0, 0]
    )
    d_tokens, gate_g, up_g, down_g = pick(places, mine, dgu, dd, gate_vals.shape[2])
    return (d_tokens, gate_g[None, None], up_g[None, None], down_g[None, None])


def solution(mesh):
    in_specs = (
        P("wide", "narrow"),
        P("wide", "narrow"),
        P("narrow", "wide", None, None, None),
        P("narrow", "wide", None, None, None),
        P("narrow", "wide", None),
        P("narrow", "wide"),
        P("wide", "narrow", None, None, None),
        P("wide", "narrow", None),
        P("wide", "narrow"),
    )
    out_specs = (
        P("wide", "narrow"),
        P("narrow", "wide", None, None, None),
        P("narrow", "wide", None, None, None),
        P("wide", "narrow", None, None, None),
    )
    return jax.shard_map(
        on_device, mesh=mesh, in_specs=in_specs, out_specs=out_specs, check_vma=False
    )
```

```python
import jax
import jax.numpy as jnp
from jax import lax
from jax.experimental import pallas as pl
from jax.experimental.pallas import tpu as pltpu
from jax.sharding import PartitionSpec as P

MESH = pl.DeviceIdType.MESH
VMEM = pl.BlockSpec(memory_space=pltpu.VMEM)
SMEM = pl.BlockSpec(memory_space=pltpu.SMEM)
F32 = jnp.float32
BF16 = jnp.bfloat16

Z = 16
N = 8
B = 128


def wide_place():
    w = lax.axis_index("wide")
    return w // 4, (w // 2) % 2, w % 2


def wide_at(z, y, c):
    return ((z + Z) % Z * 2 + y) * 2 + c


def greet(peers):
    barrier = pltpu.get_barrier_semaphore()
    for axis, peer in peers:
        pl.semaphore_signal(barrier, inc=1, device_id={axis: peer}, device_id_type=MESH)
    pl.semaphore_wait(barrier, len(peers))


def send(axis, peer, src, dst, send_sem, recv_sem):
    copy = pltpu.make_async_remote_copy(
        src_ref=src,
        dst_ref=dst,
        send_sem=send_sem,
        recv_sem=recv_sem,
        device_id={axis: peer},
        device_id_type=MESH,
    )
    copy.start()
    return copy


def tables_kernel(gu_index, gu_count, down_index, down_count, out):
    for base, index, count in ((0, gu_index, gu_count), (4, down_index, down_count)):
        live = count[0, 0]
        for block in range(16):
            out[base + 2, block] = 0
            out[base + 3, block] = 0
        for s in range(index.shape[-1]):
            at = index[0, 0, s]
            out[base, s] = at
            out[base + 1, s] = jnp.where(s < live, 1, 0)

            @pl.when(s < live)
            def _():
                out[base + 2, at] = s
                out[base + 3, at] = 1


def tables_of(*args):
    return pl.pallas_call(
        tables_kernel,
        out_shape=jax.ShapeDtypeStruct((8, 16), jnp.int32),
        in_specs=[SMEM] * 4,
        out_specs=SMEM,
        name="tables",
    )(*args)


def only_if(flag, value):
    return jnp.where(jnp.full(value.shape, flag) > 0, value.astype(F32), 0.0).astype(BF16)


ORDER = (4, 3, 5, 2, 6, 1, 7)


def layer_kernel(
    tables,
    tokens,
    cotangent,
    gate,
    up,
    down,
    out,
    dgu,
    dd,
    units,
    flat,
    wgu,
    xs,
    dys,
    wd,
    got,
    part,
    sums,
    own_sem,
    y_sem,
    z_send,
    z_recv,
    c_send,
    c_recv,
    s_send,
    s_recv,
    g_send,
    g_recv,
    *back_refs,
):
    z, y, c = wide_place()
    n = lax.axis_index("narrow")
    right, left = wide_at(z + 1, y, c), wide_at(z - 1, y, c)
    across, partner = wide_at(z, 1 - y, c), wide_at(z, y, 1 - c)
    peers = {k: (n + k) % N for k in ORDER}
    me = wide_at(z, y, c)
    owns = [
        pltpu.make_async_copy(ref, got.at[me, i], own_sem.at[i])
        for i, ref in enumerate((tokens, cotangent))
    ]
    for copy in owns:
        copy.start()
    greet([("wide", w) for w in (right, left, across, partner)] + [("narrow", p) for p in peers.values()])
    for copy in owns:
        copy.wait()
    mine = got.at[me]
    rows = (y, 1 - y)
    ycopy = send("wide", across, mine, got.at[me], y_sem.at[0], y_sem.at[1])
    sent = [ycopy]
    cores = {}
    last = {}
    reduces = {}
    shares = {}

    def ring(s, q):
        for d in (0, 1):
            steps = 8 - d
            if s > steps + 1:
                continue
            off = 1 - s if d == 0 else s - 1
            slot = wide_at(z + off, rows[q], c)
            src = got.at[slot]
            if s > 1:
                last[d, q].wait_recv()
            elif q == 1 and d == 0:
                ycopy.wait_recv()
            if s <= steps:
                k = (d * 2 + q) * 8 + s - 1
                last[d, q] = send(
                    "wide", right if d == 0 else left, src, src, z_send.at[k], z_recv.at[k]
                )
                sent.append(last[d, q])
            if s > 1 or d == 0:
                k = len(cores)
                cores[off, q] = send("wide", partner, src, src, c_send.at[k], c_recv.at[k])

    def chunk(k):
        offs = (-k, k) if k < 8 else (0, -8)
        for off in offs:
            for q in (0, 1):
                cores[off, q].wait_recv()
        slots = [wide_at(z + off, yy, cc) for off in offs for yy in (0, 1) for cc in (0, 1)]

        def rows_of(which):
            return jnp.concatenate([got[slot, which].astype(F32) for slot in slots], axis=0).astype(BF16)

        x = rows_of(0)
        xs[64 * (k - 1) : 64 * k, :] = x
        gu = jnp.dot(x, wgu[...], preferred_element_type=F32)
        part[k - 1, :, :, : 4 * B] = gu.reshape(8, 8, 4 * B)
        dy = rows_of(1)
        dys[64 * (k - 1) : 64 * k, :] = dy
        dh = lax.dot_general(dy, wd[...], (((1,), (1,)), ((), ())), preferred_element_type=F32)
        part[k - 1, :, :, 4 * B :] = dh.reshape(8, 8, 2 * B)
        for j in ORDER:
            reduces[k, j] = send(
                "narrow",
                peers[j],
                part.at[k - 1, peers[j]],
                sums.at[k - 1, j],
                s_send.at[k - 1, j],
                s_recv.at[k - 1, j],
            )

    def finish(k):
        total = part[k - 1, n]
        for j in ORDER:
            reduces[k, j].wait_recv()
            total = total + sums[k - 1, j]
        gate, up, d_hidden = total[:, : 2 * B], total[:, 2 * B : 4 * B], total[:, 4 * B :]
        sig = jax.nn.sigmoid(gate)
        units[k - 1, n, :, : 2 * B] = (gate * sig * up).astype(BF16)
        units[k - 1, n, :, 2 * B : 4 * B] = (
            d_hidden * up * sig * (1.0 + gate * (1.0 - sig))
        ).astype(BF16)
        units[k - 1, n, :, 4 * B :] = (d_hidden * gate * sig).astype(BF16)
        for j in ORDER:
            shares[k, j] = send(
                "narrow",
                peers[j],
                units.at[k - 1, n],
                units.at[k - 1, n],
                g_send.at[k - 1, j],
                g_recv.at[k - 1, j],
            )

    def settle(k):
        for j in ORDER:
            shares[k, j].wait_recv()
        flat[64 * (k - 1) : 64 * k, :] = units[k - 1].astype(F32).reshape(64, -1).astype(BF16)

    def place(table, sources, target, width):
        for block in range(16):
            row, col = block // width * B, block % width * B
            slot, flag = tables[table + 2, block], tables[table + 3, block]
            for i, source in enumerate(sources):
                at = 2 * B * i + col
                target[row : row + B, at : at + B] = only_if(flag, source[slot])

    for i in range(1, 11):
        if i <= 9:
            ring(i, 0)
        if i == 1:
            place(0, (gate, up), wgu, 2)
            place(4, (down,), wd, 8)
        else:
            ring(i - 1, 1)
        if i > 2:
            chunk(i - 2)
        if i > 3:
            finish(i - 3)
        if i > 5:
            settle(i - 5)
    finish(8)
    for k in (6, 7, 8):
        settle(k)
    back(flat, wgu, xs, dys, out, dgu, dd, *back_refs)
    for group in (cores, reduces, shares):
        sent.extend(group.values())
    for copy in sent:
        copy.wait_send()


def chunk_of(off):
    if off in (0, 8):
        return 7, (off == 8) * 1
    return abs(off) - 1, (off > 0) * 1


def back(
    units, wgu, xs, dys, out, dgu, dd, part, held, run, last, c_send, c_recv, z_send, z_recv, y_sem
):
    z, y, c = wide_place()
    right, left = wide_at(z + 1, y, c), wide_at(z - 1, y, c)
    across, partner = wide_at(z, 1 - y, c), wide_at(z, y, 1 - c)
    rows = (1 - y, y)
    cores = {}

    def terms(s):
        offs = (8 - s, s - 7)
        places = [chunk_of(off) for off in offs]
        picked = jnp.concatenate(
            [units[64 * k + 32 * j : 64 * k + 32 * (j + 1), 2 * B :] for k, j in places], axis=0
        )
        dx = lax.dot_general(
            picked, wgu[...], (((1,), (1,)), ((), ())), preferred_element_type=F32
        ).reshape(2, 2, 2, 8, -1)
        for i, (k, j) in enumerate(places):
            part[k, j] = dx[i]
            a = 2 * s + i
            cores[offs[i]] = send(
                "wide", partner, part.at[k, j, :, 1 - c], held.at[k, j], c_send.at[a], c_recv.at[a]
            )

    def mine(off, q):
        k, j = chunk_of(off)
        return part[k, j, rows[q], c] + held[k, j, rows[q]]

    def across_tokens(a, b):
        return lax.dot_general(
            a, b, (((0,), (0,)), ((), ())), preferred_element_type=F32
        ).astype(BF16)

    def gradients(s):
        if s < 4:
            dense = across_tokens(xs[:, 2 * B * s : 2 * B * (s + 1)], units[:, 2 * B :])
            for row in (0, 1):
                for i in (0, 1):
                    for col in (0, 1):
                        at = B * (2 * i + col)
                        dgu[i, 2 * (2 * s + row) + col] = dense[row * B : (row + 1) * B, at : at + B]
        elif s < 6:
            half = s - 4
            dense = across_tokens(units[:, : 2 * B], dys[:, 4 * B * half : 4 * B * (half + 1)])
            for row in (0, 1):
                for col in range(4):
                    dd[8 * row + 4 * half + col] = dense[row * B : (row + 1) * B, col * B : (col + 1) * B]

    prev = {}
    sent = []
    terms(0)
    terms(1)

    def step(s, q):
        for d in (0, 1):
            if s >= 8 - d:
                continue
            off = 8 - s if d == 0 else s - 7
            if q == 0:
                cores[off].wait_recv()
            if s == 0:
                run[d, q, s] = mine(off, q)
            else:
                prev[d, q].wait_recv()
                run[d, q, s] = run[d, q, s] + mine(off, q)
            k = (d * 2 + q) * 8 + s
            prev[d, q] = send(
                "wide",
                right if d == 0 else left,
                run.at[d, q, s],
                run.at[d, q, s + 1],
                z_send.at[k],
                z_recv.at[k],
            )
            sent.append(prev[d, q])

    for i in range(9):
        if i < 8:
            step(i, 0)
        if i > 0:
            step(i - 1, 1)
        if i + 2 < 8:
            terms(i + 2)
        if 2 <= i < 8:
            gradients(i - 2)
    cores[0].wait_recv()

    def total(q):
        prev[1, q].wait_recv()
        left_sum = run[1, q, 7] + mine(0, q)
        prev[0, q].wait_recv()
        return left_sum + run[0, q, 8]

    last[0] = total(0)
    ycopy = send("wide", across, last.at[0], last.at[1], y_sem.at[0], y_sem.at[1])
    own = total(1)
    ycopy.wait_recv()
    out[...] = (own + last[1]).astype(BF16)
    for copy in sent + list(cores.values()) + [ycopy]:
        copy.wait_send()


def layer(tables, tokens, cotangent, gate, up, down):
    width = tokens.shape[-1]
    sem = pltpu.SemaphoreType.DMA
    return pl.pallas_call(
        layer_kernel,
        out_shape=(
            jax.ShapeDtypeStruct((8, width), BF16),
            jax.ShapeDtypeStruct((2, 16, B, B), BF16),
            jax.ShapeDtypeStruct((16, B, B), BF16),
        ),
        in_specs=[SMEM] + [VMEM] * 5,
        out_specs=(VMEM,) * 3,
        scratch_shapes=[
            pltpu.VMEM((8, N, 8, 6 * B), BF16),
            pltpu.VMEM((512, 6 * B), BF16),
            pltpu.VMEM((8 * B, 4 * B), BF16),
            pltpu.VMEM((512, width), BF16),
            pltpu.VMEM((512, width), BF16),
            pltpu.VMEM((2 * B, 8 * B), BF16),
            pltpu.VMEM((4 * Z, 2, 8, width), BF16),
            pltpu.VMEM((8, N, 8, 6 * B), F32),
            pltpu.VMEM((8, N, 8, 6 * B), F32),
            sem((2,)),
            sem((2,)),
            sem((32,)),
            sem((32,)),
            sem((32,)),
            sem((32,)),
            sem((8, N)),
            sem((8, N)),
            sem((8, N)),
            sem((8, N)),
            pltpu.VMEM((8, 2, 2, 2, 8, width), F32),
            pltpu.VMEM((8, 2, 2, 8, width), F32),
            pltpu.VMEM((2, 2, 9, 8, width), F32),
            pltpu.VMEM((2, 8, width), F32),
            sem((Z,)),
            sem((Z,)),
            sem((32,)),
            sem((32,)),
            sem((2,)),
        ],
        compiler_params=pltpu.CompilerParams(collective_id=0, has_side_effects=True),
        name="layer",
    )(tables, tokens, cotangent, gate, up, down)


def pick_kernel(gu_index, gu_count, down_index, down_count, mine, dgu, dd, out, gate_g, up_g, down_g):
    out[...] = mine[...]
    for s in range(gate_g.shape[0]):
        alive = s < gu_count[0, 0]

        @pl.when(alive)
        def _():
            at = gu_index[0, 0, s]
            gate_g[s] = dgu[0, at]
            up_g[s] = dgu[1, at]

        @pl.when(jnp.logical_not(alive))
        def _():
            gate_g[s] = jnp.zeros((B, B), BF16)
            up_g[s] = jnp.zeros((B, B), BF16)

        d_alive = s < down_count[0, 0]

        @pl.when(d_alive)
        def _():
            down_g[s] = dd[down_index[0, 0, s]]

        @pl.when(jnp.logical_not(d_alive))
        def _():
            down_g[s] = jnp.zeros((B, B), BF16)


def pick(places, mine, dgu, dd, slots):
    grad = jax.ShapeDtypeStruct((slots, B, B), BF16)
    return pl.pallas_call(
        pick_kernel,
        out_shape=(jax.ShapeDtypeStruct(mine.shape, BF16), grad, grad, grad),
        in_specs=[SMEM] * 4 + [VMEM] * 3,
        out_specs=(VMEM,) * 4,
        name="pick",
    )(*places, mine, dgu, dd)


def on_device(
    tokens, cotangent, gate_vals, up_vals, gu_index, gu_count, down_vals, down_index, down_count
):
    places = (gu_index, gu_count, down_index, down_count)
    mine, dgu, dd = layer(
        tables_of(*places), tokens, cotangent, gate_vals[0, 0], up_vals[0, 0], down_vals[0, 0]
    )
    d_tokens, gate_g, up_g, down_g = pick(places, mine, dgu, dd, gate_vals.shape[2])
    return (d_tokens, gate_g[None, None], up_g[None, None], down_g[None, None])


def solution(mesh):
    in_specs = (
        P("wide", "narrow"),
        P("wide", "narrow"),
        P("narrow", "wide", None, None, None),
        P("narrow", "wide", None, None, None),
        P("narrow", "wide", None),
        P("narrow", "wide"),
        P("wide", "narrow", None, None, None),
        P("wide", "narrow", None),
        P("wide", "narrow"),
    )
    out_specs = (
        P("wide", "narrow"),
        P("narrow", "wide", None, None, None),
        P("narrow", "wide", None, None, None),
        P("wide", "narrow", None, None, None),
    )
    return jax.shard_map(
        on_device, mesh=mesh, in_specs=in_specs, out_specs=out_specs, check_vma=False
    )
```

```python
import jax
import jax.numpy as jnp
from jax import lax
from jax.experimental import pallas as pl
from jax.experimental.pallas import tpu as pltpu
from jax.sharding import PartitionSpec as P

MESH = pl.DeviceIdType.MESH
VMEM = pl.BlockSpec(memory_space=pltpu.VMEM)
SMEM = pl.BlockSpec(memory_space=pltpu.SMEM)
F32 = jnp.float32
BF16 = jnp.bfloat16

Z = 16
N = 8
B = 128


def wide_place():
    w = lax.axis_index("wide")
    return w // 4, (w // 2) % 2, w % 2


def wide_at(z, y, c):
    return ((z + Z) % Z * 2 + y) * 2 + c


def greet(peers):
    barrier = pltpu.get_barrier_semaphore()
    for axis, peer in peers:
        pl.semaphore_signal(barrier, inc=1, device_id={axis: peer}, device_id_type=MESH)
    pl.semaphore_wait(barrier, len(peers))


def send(axis, peer, src, dst, send_sem, recv_sem):
    copy = pltpu.make_async_remote_copy(
        src_ref=src,
        dst_ref=dst,
        send_sem=send_sem,
        recv_sem=recv_sem,
        device_id={axis: peer},
        device_id_type=MESH,
    )
    copy.start()
    return copy


def tables_kernel(gu_index, gu_count, down_index, down_count, out):
    for base, index, count in ((0, gu_index, gu_count), (4, down_index, down_count)):
        live = count[0, 0]
        for block in range(16):
            out[base + 2, block] = 0
            out[base + 3, block] = 0
        for s in range(index.shape[-1]):
            at = index[0, 0, s]
            out[base, s] = at
            out[base + 1, s] = jnp.where(s < live, 1, 0)

            @pl.when(s < live)
            def _():
                out[base + 2, at] = s
                out[base + 3, at] = 1


def tables_of(*args):
    return pl.pallas_call(
        tables_kernel,
        out_shape=jax.ShapeDtypeStruct((8, 16), jnp.int32),
        in_specs=[SMEM] * 4,
        out_specs=SMEM,
        name="tables",
    )(*args)


def only_if(flag, value):
    return jnp.where(jnp.full(value.shape, flag) > 0, value.astype(F32), 0.0).astype(BF16)


ORDER = (4, 3, 5, 2, 6, 1, 7)


def layer_kernel(
    tables,
    tokens,
    cotangent,
    gate,
    up,
    down,
    out,
    dgu,
    dd,
    units,
    flat,
    wgu,
    xs,
    dys,
    wd,
    got,
    part,
    sums,
    own_sem,
    y_sem,
    z_send,
    z_recv,
    c_send,
    c_recv,
    s_send,
    s_recv,
    g_send,
    g_recv,
    *back_refs,
):
    z, y, c = wide_place()
    n = lax.axis_index("narrow")
    right, left = wide_at(z + 1, y, c), wide_at(z - 1, y, c)
    across, partner = wide_at(z, 1 - y, c), wide_at(z, y, 1 - c)
    peers = {k: (n + k) % N for k in ORDER}
    me = wide_at(z, y, c)
    owns = [
        pltpu.make_async_copy(ref, got.at[me, i], own_sem.at[i])
        for i, ref in enumerate((tokens, cotangent))
    ]
    for copy in owns:
        copy.start()
    greet([("wide", w) for w in (right, left, across, partner)] + [("narrow", p) for p in peers.values()])
    for copy in owns:
        copy.wait()
    mine = got.at[me]
    rows = (y, 1 - y)
    ycopy = send("wide", across, mine, got.at[me], y_sem.at[0], y_sem.at[1])
    sent = [ycopy]
    cores = {}
    last = {}
    reduces = {}
    shares = {}

    def ring(s, q):
        for d in (0, 1):
            steps = 8 - d
            if s > steps + 1:
                continue
            off = 1 - s if d == 0 else s - 1
            slot = wide_at(z + off, rows[q], c)
            src = got.at[slot]
            if s > 1:
                last[d, q].wait_recv()
            elif q == 1 and d == 0:
                ycopy.wait_recv()
            if s <= steps:
                k = (d * 2 + q) * 8 + s - 1
                last[d, q] = send(
                    "wide", right if d == 0 else left, src, src, z_send.at[k], z_recv.at[k]
                )
                sent.append(last[d, q])
            if s > 1 or d == 0:
                k = len(cores)
                cores[off, q] = send("wide", partner, src, src, c_send.at[k], c_recv.at[k])

    def chunk(k):
        offs = (-k, k) if k < 8 else (0, -8)
        for off in offs:
            for q in (0, 1):
                cores[off, q].wait_recv()
        slots = [wide_at(z + off, yy, cc) for off in offs for yy in (0, 1) for cc in (0, 1)]

        def rows_of(which):
            return jnp.concatenate([got[slot, which].astype(F32) for slot in slots], axis=0).astype(BF16)

        x = rows_of(0)
        xs[64 * (k - 1) : 64 * k, :] = x
        gu = jnp.dot(x, wgu[...], preferred_element_type=F32)
        part[k - 1, :, :, : 4 * B] = gu.reshape(8, 8, 4 * B)
        dy = rows_of(1)
        dys[64 * (k - 1) : 64 * k, :] = dy
        dh = lax.dot_general(dy, wd[...], (((1,), (1,)), ((), ())), preferred_element_type=F32)
        part[k - 1, :, :, 4 * B :] = dh.reshape(8, 8, 2 * B)
        for j in ORDER:
            reduces[k, j] = send(
                "narrow",
                peers[j],
                part.at[k - 1, peers[j]],
                sums.at[k - 1, j],
                s_send.at[k - 1, j],
                s_recv.at[k - 1, j],
            )

    def finish(k):
        total = part[k - 1, n]
        for j in ORDER:
            reduces[k, j].wait_recv()
            total = total + sums[k - 1, j]
        gate, up, d_hidden = total[:, : 2 * B], total[:, 2 * B : 4 * B], total[:, 4 * B :]
        sig = jax.nn.sigmoid(gate)
        units[k - 1, n, :, : 2 * B] = (gate * sig * up).astype(BF16)
        units[k - 1, n, :, 2 * B : 4 * B] = (
            d_hidden * up * sig * (1.0 + gate * (1.0 - sig))
        ).astype(BF16)
        units[k - 1, n, :, 4 * B :] = (d_hidden * gate * sig).astype(BF16)
        for j in ORDER:
            shares[k, j] = send(
                "narrow",
                peers[j],
                units.at[k - 1, n],
                units.at[k - 1, n],
                g_send.at[k - 1, j],
                g_recv.at[k - 1, j],
            )

    def settle(k):
        for j in ORDER:
            shares[k, j].wait_recv()
        flat[64 * (k - 1) : 64 * k, :] = units[k - 1].astype(F32).reshape(64, -1).astype(BF16)

    def place(table, sources, target, width):
        for block in range(16):
            row, col = block // width * B, block % width * B
            slot, flag = tables[table + 2, block], tables[table + 3, block]
            for i, source in enumerate(sources):
                at = 2 * B * i + col
                target[row : row + B, at : at + B] = only_if(flag, source[slot])

    for i in range(1, 11):
        if i <= 9:
            ring(i, 0)
        if i == 1:
            place(0, (gate, up), wgu, 2)
            place(4, (down,), wd, 8)
        else:
            ring(i - 1, 1)
        if i > 2:
            chunk(i - 2)
        if i > 4:
            finish(i - 4)
        if i > 6:
            settle(i - 6)
    finish(7)
    finish(8)
    for k in (5, 6, 7, 8):
        settle(k)
    back(flat, wgu, xs, dys, out, dgu, dd, *back_refs)
    for group in (cores, reduces, shares):
        sent.extend(group.values())
    for copy in sent:
        copy.wait_send()


def chunk_of(off):
    if off in (0, 8):
        return 7, (off == 8) * 1
    return abs(off) - 1, (off > 0) * 1


def back(
    units, wgu, xs, dys, out, dgu, dd, part, held, run, last, c_send, c_recv, z_send, z_recv, y_sem
):
    z, y, c = wide_place()
    right, left = wide_at(z + 1, y, c), wide_at(z - 1, y, c)
    across, partner = wide_at(z, 1 - y, c), wide_at(z, y, 1 - c)
    rows = (1 - y, y)
    cores = {}

    def terms(s):
        offs = (8 - s, s - 7)
        places = [chunk_of(off) for off in offs]
        picked = jnp.concatenate(
            [units[64 * k + 32 * j : 64 * k + 32 * (j + 1), 2 * B :] for k, j in places], axis=0
        )
        dx = lax.dot_general(
            picked, wgu[...], (((1,), (1,)), ((), ())), preferred_element_type=F32
        ).reshape(2, 2, 2, 8, -1)
        for i, (k, j) in enumerate(places):
            part[k, j] = dx[i]
            a = 2 * s + i
            cores[offs[i]] = send(
                "wide", partner, part.at[k, j, :, 1 - c], held.at[k, j], c_send.at[a], c_recv.at[a]
            )

    def mine(off, q):
        k, j = chunk_of(off)
        return part[k, j, rows[q], c] + held[k, j, rows[q]]

    def across_tokens(a, b):
        return lax.dot_general(
            a, b, (((0,), (0,)), ((), ())), preferred_element_type=F32
        ).astype(BF16)

    def gradients(s):
        if s < 4:
            dense = across_tokens(xs[:, 2 * B * s : 2 * B * (s + 1)], units[:, 2 * B :])
            for row in (0, 1):
                for i in (0, 1):
                    for col in (0, 1):
                        at = B * (2 * i + col)
                        dgu[i, 2 * (2 * s + row) + col] = dense[row * B : (row + 1) * B, at : at + B]
        elif s < 6:
            half = s - 4
            dense = across_tokens(units[:, : 2 * B], dys[:, 4 * B * half : 4 * B * (half + 1)])
            for row in (0, 1):
                for col in range(4):
                    dd[8 * row + 4 * half + col] = dense[row * B : (row + 1) * B, col * B : (col + 1) * B]

    prev = {}
    sent = []
    terms(0)
    terms(1)

    def step(s, q):
        for d in (0, 1):
            if s >= 8 - d:
                continue
            off = 8 - s if d == 0 else s - 7
            if q == 0:
                cores[off].wait_recv()
            if s == 0:
                run[d, q, s] = mine(off, q)
            else:
                prev[d, q].wait_recv()
                run[d, q, s] = run[d, q, s] + mine(off, q)
            k = (d * 2 + q) * 8 + s
            prev[d, q] = send(
                "wide",
                right if d == 0 else left,
                run.at[d, q, s],
                run.at[d, q, s + 1],
                z_send.at[k],
                z_recv.at[k],
            )
            sent.append(prev[d, q])

    for i in range(9):
        if i < 8:
            step(i, 0)
        if i > 0:
            step(i - 1, 1)
        if i + 2 < 8:
            terms(i + 2)
        if 2 <= i < 8:
            gradients(i - 2)
    cores[0].wait_recv()

    def total(q):
        prev[1, q].wait_recv()
        left_sum = run[1, q, 7] + mine(0, q)
        prev[0, q].wait_recv()
        return left_sum + run[0, q, 8]

    last[0] = total(0)
    ycopy = send("wide", across, last.at[0], last.at[1], y_sem.at[0], y_sem.at[1])
    own = total(1)
    ycopy.wait_recv()
    out[...] = (own + last[1]).astype(BF16)
    for copy in sent + list(cores.values()) + [ycopy]:
        copy.wait_send()


def layer(tables, tokens, cotangent, gate, up, down):
    width = tokens.shape[-1]
    sem = pltpu.SemaphoreType.DMA
    return pl.pallas_call(
        layer_kernel,
        out_shape=(
            jax.ShapeDtypeStruct((8, width), BF16),
            jax.ShapeDtypeStruct((2, 16, B, B), BF16),
            jax.ShapeDtypeStruct((16, B, B), BF16),
        ),
        in_specs=[SMEM] + [VMEM] * 5,
        out_specs=(VMEM,) * 3,
        scratch_shapes=[
            pltpu.VMEM((8, N, 8, 6 * B), BF16),
            pltpu.VMEM((512, 6 * B), BF16),
            pltpu.VMEM((8 * B, 4 * B), BF16),
            pltpu.VMEM((512, width), BF16),
            pltpu.VMEM((512, width), BF16),
            pltpu.VMEM((2 * B, 8 * B), BF16),
            pltpu.VMEM((4 * Z, 2, 8, width), BF16),
            pltpu.VMEM((8, N, 8, 6 * B), F32),
            pltpu.VMEM((8, N, 8, 6 * B), F32),
            sem((2,)),
            sem((2,)),
            sem((32,)),
            sem((32,)),
            sem((32,)),
            sem((32,)),
            sem((8, N)),
            sem((8, N)),
            sem((8, N)),
            sem((8, N)),
            pltpu.VMEM((8, 2, 2, 2, 8, width), F32),
            pltpu.VMEM((8, 2, 2, 8, width), F32),
            pltpu.VMEM((2, 2, 9, 8, width), F32),
            pltpu.VMEM((2, 8, width), F32),
            sem((Z,)),
            sem((Z,)),
            sem((32,)),
            sem((32,)),
            sem((2,)),
        ],
        compiler_params=pltpu.CompilerParams(collective_id=0, has_side_effects=True),
        name="layer",
    )(tables, tokens, cotangent, gate, up, down)


def pick_kernel(gu_index, gu_count, down_index, down_count, mine, dgu, dd, out, gate_g, up_g, down_g):
    out[...] = mine[...]
    for s in range(gate_g.shape[0]):
        alive = s < gu_count[0, 0]

        @pl.when(alive)
        def _():
            at = gu_index[0, 0, s]
            gate_g[s] = dgu[0, at]
            up_g[s] = dgu[1, at]

        @pl.when(jnp.logical_not(alive))
        def _():
            gate_g[s] = jnp.zeros((B, B), BF16)
            up_g[s] = jnp.zeros((B, B), BF16)

        d_alive = s < down_count[0, 0]

        @pl.when(d_alive)
        def _():
            down_g[s] = dd[down_index[0, 0, s]]

        @pl.when(jnp.logical_not(d_alive))
        def _():
            down_g[s] = jnp.zeros((B, B), BF16)


def pick(places, mine, dgu, dd, slots):
    grad = jax.ShapeDtypeStruct((slots, B, B), BF16)
    return pl.pallas_call(
        pick_kernel,
        out_shape=(jax.ShapeDtypeStruct(mine.shape, BF16), grad, grad, grad),
        in_specs=[SMEM] * 4 + [VMEM] * 3,
        out_specs=(VMEM,) * 4,
        name="pick",
    )(*places, mine, dgu, dd)


def on_device(
    tokens, cotangent, gate_vals, up_vals, gu_index, gu_count, down_vals, down_index, down_count
):
    places = (gu_index, gu_count, down_index, down_count)
    mine, dgu, dd = layer(
        tables_of(*places), tokens, cotangent, gate_vals[0, 0], up_vals[0, 0], down_vals[0, 0]
    )
    d_tokens, gate_g, up_g, down_g = pick(places, mine, dgu, dd, gate_vals.shape[2])
    return (d_tokens, gate_g[None, None], up_g[None, None], down_g[None, None])


def solution(mesh):
    in_specs = (
        P("wide", "narrow"),
        P("wide", "narrow"),
        P("narrow", "wide", None, None, None),
        P("narrow", "wide", None, None, None),
        P("narrow", "wide", None),
        P("narrow", "wide"),
        P("wide", "narrow", None, None, None),
        P("wide", "narrow", None),
        P("wide", "narrow"),
    )
    out_specs = (
        P("wide", "narrow"),
        P("narrow", "wide", None, None, None),
        P("narrow", "wide", None, None, None),
        P("wide", "narrow", None, None, None),
    )
    return jax.shard_map(
        on_device, mesh=mesh, in_specs=in_specs, out_specs=out_specs, check_vma=False
    )
```
